256 devices in a mesh: blk: 64 (over y, z_hi, x), tp: 4 (over z_lo, core).
Axes of the slice: x: 4, y: 4, z: 8 (z_hi: 4, z_lo: 2; z = z_hi * 2 + z_lo), core: 2. Of those that a mesh axis runs over, the one named last changes fastest.
Arguments:
- hidden_in: bfloat16 [8192, 5120], P(('blk', 'tp')), may hold values from -6 to 6
- norm_gain: bfloat16 [5120], replicated, may hold values from 0.099609375 to 1.8984375
- kv_weight: bfloat16 [5120, 2, 1024], P(None, None, 'tp'), may hold values from -0.078125 to 0.078125
- kv_bias: bfloat16 [2, 1024], P(None, 'tp'), may hold values from -3 to 3
- queries: bfloat16 [8192, 5120], P('blk', 'tp'), may hold values from -110 to 110
- cache_pages: bfloat16 [64, 128, 2, 8, 128], P('blk', None, None, 'tp'), may hold values from -6 to 6
- out_weight: bfloat16 [5120, 5120], P('tp', 'blk'), may hold values from -0.3125 to 0.3125
- cached_len: int32 [64], replicated, may hold values from 0 to 4096
- page_table: int32 [64, 32], replicated, may hold values from 0 to 63, as said below
Outputs:
- hidden_out: bfloat16 [8192, 5120], P(('blk', 'tp'))
- new_kv: bfloat16 [8192, 2, 8, 128], P('blk', None, 'tp')
The draws below stay inside these ranges and needn't reach their ends.
Inputs may be any that keep to these rules, and one draw needn't show every extreme that they name: `page_table`: request r's cache fills its first ceil(cached_len[r] / 128) page table entries with distinct physical pages, no page serving two requests; later entries are 0. One request holds exactly 4096 tokens.
All inputs are finite; a program needn't handle non-finite values.
Results may differ from the reference program's by a relative error of at most 0.012.
The reference program's roundings to bfloat16 on the way count: a program that leaves them out, or rounds other values in their place, can miss the bound.
Values may be sent and summed in bfloat16 or wider, within the bound.
A program may use at most 128 MiB of HBM per device.

```python
import jax
import jax.numpy as jnp
from jax import lax

D = 5120
H = 40
KVH = 8
HD = 128
PAGE = 128
TOK_DEV = 128
TOKENS = 8192
REQS = 64
NPAGES = 64
MAXPAGES = 32
N_TP = 4


def page_layout(key):
    key_one, key_two, key_three, key_four = jax.random.split(jax.random.fold_in(key, 11), 4)
    shares = jax.random.randint(key_one, (REQS,), 1, 9) ** 2
    largest = jax.random.randint(key_two, (), 0, REQS)
    is_largest = jnp.arange(REQS) == largest
    spare = NPAGES - MAXPAGES
    base_each = 1 if spare >= REQS - 1 else 0
    remaining = spare - base_each * (REQS - 1)
    weighted = jnp.where(is_largest, 0, shares)
    extra = base_each + jnp.minimum(remaining * weighted // jnp.sum(weighted), MAXPAGES - base_each)
    page_count = jnp.where(is_largest, MAXPAGES, extra)
    offsets = jax.random.randint(key_three, (REQS,), 1, PAGE + 1)
    offsets = jnp.where(is_largest, PAGE, offsets)
    lengths = jnp.where(page_count > 0, (page_count - 1) * PAGE + offsets, 0)
    shuffled = jax.random.permutation(key_four, NPAGES)
    starts = jnp.cumsum(page_count) - page_count
    slot_ids = jnp.arange(MAXPAGES)
    slots = jnp.clip(starts[:, None] + slot_ids[None, :], 0, NPAGES - 1)
    table = jnp.where(slot_ids[None, :] < page_count[:, None], shuffled[slots], 0)
    return (lengths.astype(jnp.int32), table.astype(jnp.int32))


def draw_cached_len(key, part):
    return page_layout(key)[0]


def draw_page_table(key, part):
    return page_layout(key)[1]


def draw_queries(key, part):
    key_two = jax.random.fold_in(jax.random.fold_in(key, 5), 1)
    values = jnp.clip(jax.random.normal(key_two, (TOKENS, H * HD), jnp.float32), -6.0, 6.0)
    return values.astype(jnp.bfloat16)


def block_levels(rng, extent, shards, least, high):
    factor_of = 1.0
    for dim, parts in shards:
        heights = jax.random.uniform(jax.random.fold_in(jax.random.fold_in(rng, 6), dim), (parts,), jnp.float32, least / len(shards), high / len(shards))
        factor_of = factor_of * jnp.repeat(jnp.exp(heights), extent[dim] // parts).reshape((-1,) + (1,) * (len(extent) - 1 - dim))
    return factor_of


def noise(own_key, shape, spread, most, cuts=(), held_as=jnp.bfloat16):
    entries = jax.random.normal(own_key, shape, jnp.float32) * spread
    if len(cuts) > 0:
        entries = block_levels(own_key, shape, cuts, -0.22, 0.18) * entries
    return jnp.clip(entries, min=-most, max=most).astype(held_as)


def setup_inputs(seed: int = 0) -> dict:
    key_list = jax.random.split(jax.random.key(seed), 10)
    return {
        "hidden_in": noise(key_list[0], (TOKENS, D), 1.0, 6.0, ((0, 256),)),
        "norm_gain": jnp.clip(1.0 + 0.18 * jax.random.normal(key_list[1], (D,), jnp.float32), 0.099609375, 1.8984375).astype(jnp.bfloat16),
        "kv_weight": noise(key_list[2], (D, 2, KVH * HD), D ** -0.5, 0.078125, ((2, 4),)),
        "kv_bias": noise(key_list[3], (2, KVH * HD), 0.5, 3.0, ((1, 4),)),
        "queries": draw_queries(jax.random.fold_in(key_list[9], 71), 0),
        "cache_pages": noise(key_list[5], (NPAGES, PAGE, 2, KVH, HD), 1.0, 6.0, ((0, 64), (3, 4))),
        "out_weight": noise(key_list[6], (H * HD, D), (H * HD // 16) ** -0.5, 0.3125, ((0, 4), (1, 64))),
        "cached_len": draw_cached_len(jax.random.fold_in(key_list[9], 71), 0),
        "page_table": draw_page_table(jax.random.fold_in(key_list[9], 71), 0),
    }


EPS = 1e-06
THETA = 1000000.0

def rotate(values, positions, head_dim):
    half_dim = head_dim // 2
    inverse = jnp.power(THETA, -jnp.arange(half_dim, dtype=jnp.float32) * 2.0 / head_dim)
    angles = positions[:, None] * inverse[None, :]
    cosine = jnp.cos(angles)[:, None, :]
    sine_val = jnp.sin(angles)[:, None, :]
    front_half = values[..., :half_dim]
    back_half = values[..., half_dim:]
    return jnp.concatenate([front_half * cosine - back_half * sine_val, back_half * cosine + front_half * sine_val], axis=-1)

def reference(hidden_in, norm_gain, kv_weight, kv_bias, queries, cache_pages, out_weight, cached_len, page_table):
    hidden_f = hidden_in.astype(jnp.float32)
    inverse_rms = lax.rsqrt(lax.optimization_barrier(jnp.mean(hidden_f * hidden_f, axis=-1, keepdims=True)) + EPS)
    normed = (hidden_f * inverse_rms * norm_gain.astype(jnp.float32)).astype(jnp.bfloat16)
    token_ids = jnp.arange(TOKENS, dtype=jnp.int32)
    owners = token_ids // TOK_DEV
    positions = (cached_len[owners] + token_ids % TOK_DEV).astype(jnp.float32)
    projected = jnp.einsum('td,dsc->tsc', normed.astype(jnp.float32), kv_weight.astype(jnp.float32))
    projected = (projected + kv_bias.astype(jnp.float32)).reshape(TOKENS, 2, KVH, HD)
    key_rot = rotate(projected[:, 0], positions, HD)
    new_kv = jnp.stack([key_rot, projected[:, 1]], axis=1).astype(jnp.bfloat16)
    query_rot = rotate(queries.astype(jnp.float32).reshape(TOKENS, H, HD), positions, HD).astype(jnp.bfloat16)
    group_size = H // KVH
    score_scale = HD ** (-0.5)
    cache_rows = MAXPAGES * PAGE

    def one_request(request):
        query_part = lax.dynamic_slice_in_dim(query_rot, request * TOK_DEV, TOK_DEV, 0).reshape(TOK_DEV, KVH, group_size, HD)
        new_part = lax.dynamic_slice_in_dim(new_kv, request * TOK_DEV, TOK_DEV, 0)
        page_rows = cache_pages[page_table[request]].reshape(cache_rows, 2, KVH, HD)
        every_key = jnp.concatenate([page_rows, new_part], axis=0)
        cached_ok = jnp.arange(cache_rows, dtype=jnp.int32) < cached_len[request]
        span_ids = jnp.arange(TOK_DEV, dtype=jnp.int32)
        causal = span_ids[None, :] <= span_ids[:, None]
        visible = jnp.concatenate([jnp.broadcast_to(cached_ok[None, :], (TOK_DEV, cache_rows)), causal], axis=1)
        scores = jnp.einsum('tkgd,nkd->kgtn', query_part.astype(jnp.float32), every_key[:, 0].astype(jnp.float32)) * score_scale
        masked = jnp.where(visible[None, None], scores, -jnp.inf)
        row_max = lax.optimization_barrier(jnp.max(masked, axis=-1, keepdims=True))
        weights = jnp.exp(masked - row_max)
        row_sum = lax.optimization_barrier(jnp.sum(weights, axis=-1))
        probs = weights.astype(jnp.bfloat16)
        mixed = jnp.einsum('kgtn,nkd->kgtd', probs.astype(jnp.float32), every_key[:, 1].astype(jnp.float32))
        mixed = mixed / row_sum[..., None]
        return mixed.transpose(2, 0, 1, 3).reshape(TOK_DEV, H * HD).astype(jnp.bfloat16)
    attended = lax.map(one_request, jnp.arange(REQS, dtype=jnp.int32)).reshape(TOKENS, H * HD)
    group_cols = H * HD // N_TP
    summed = jnp.zeros((TOKENS, D), jnp.float32)
    for column_group in range(N_TP):
        partial_term = jnp.dot(attended[:, column_group * group_cols:(column_group + 1) * group_cols], out_weight[column_group * group_cols:(column_group + 1) * group_cols], preferred_element_type=jnp.float32)
        rounded = lax.optimization_barrier(partial_term.astype(jnp.bfloat16))
        summed = summed + rounded.astype(jnp.float32)
    hidden_out = (hidden_f + summed).astype(jnp.bfloat16)
    return (hidden_out, new_kv)
```

```python
import functools

import jax
import jax.numpy as jnp
from jax import lax
from jax.experimental import pallas as pl
from jax.experimental.pallas import tpu as pltpu
from jax.sharding import Mesh, PartitionSpec as P

EPS = 1e-06
THETA = 1000000.0
LOW = -1e30
LOG2E = 1.4426950408889634
MESH = pl.DeviceIdType.MESH
HBM = pl.ANY
BF = jnp.bfloat16


def coords():
    return tuple(lax.axis_index(a) for a in ("y", "zh", "x", "zl", "c"))


def shifted(axis, by):
    me = list(coords())
    me[axis] = lax.rem(me[axis] + by + 4, 4)
    return tuple(me)


def remote(src, dst, sems, n, device):
    return pltpu.make_async_remote_copy(
        src_ref=src, dst_ref=dst, send_sem=sems.at[0, n], recv_sem=sems.at[1, n],
        device_id=device, device_id_type=MESH)


class Ring:
    def __init__(self, me, peer, own, at, half, sems, base):
        self.me, self.peer, self.own, self.at, self.half = me, peer, own, at, half
        self.sems, self.base = sems, base
        self.sent = []

    def slot(self, r):
        return lax.rem(self.me + r + 4, 4)

    def part(self, s, h):
        return self.at(s).at[pl.ds(h * self.half, self.half)]

    def start(self):
        for n, by in ((0, 1), (1, -1)):
            d = remote(self.own, self.at(self.me), self.sems, self.base + n, self.peer(by))
            d.start()
            self.sent.append(d)

    def arrived(self, r):
        n = 0 if r == -1 else 1
        s = self.at(self.slot(r))
        remote(s, s, self.sems, self.base + n, self.peer(1)).wait_recv()

    def forward(self, r):
        h = 0 if r == -1 else 1
        s = self.part(self.slot(r), h)
        d = remote(s, s, self.sems, self.base + 2 + h, self.peer(-r))
        d.start()
        self.sent.append(d)

    def far(self):
        for h in (0, 1):
            s = self.part(self.slot(2), h)
            remote(s, s, self.sems, self.base + 2 + h, self.peer(1)).wait_recv()

    def drain(self):
        for d in self.sent:
            d.wait_send()


def gather_kernel(rows_ref, pages_ref, q_ref, w_ref, rows_all, py, px, qy, qx, w4, sems, lsem):
    y, zh, x, zl, c = coords()
    partner = (y, zh, x, zl, 1 - c)
    across = (y, zh, x, 1 - zl, c)
    barrier = pltpu.get_barrier_semaphore()
    near = [shifted(a, b) for a in (0, 1, 2) for b in (1, -1)] + [partner, across]
    for d in near:
        pl.semaphore_signal(barrier, inc=1, device_id=d, device_id_type=MESH)
    pl.semaphore_wait(barrier, len(near))

    tp = 2 * zl + c
    base = [0]

    def new(me, peer, own, at, half, count=4):
        r = Ring(me, peer, own, at, half, sems, base[0])
        base[0] += count
        return r

    peer_z = lambda by: shifted(1, by)
    peer_y = lambda by: shifted(0, by)
    peer_x = lambda by: shifted(2, by)

    def w_slot(i):
        t = lax.rem(i, 2)
        return w4.at[t, i // 2, x * (1 - t) + y * t]

    def w_ring(r):
        i = lax.rem(zh + r + 4, 4)
        t = lax.rem(i, 2)
        def peer(by):
            return (lax.rem(y + t * by + 4, 4), zh, lax.rem(x + (1 - t) * by + 4, 4), zl, c)
        own = w_ref if r == 0 else w_slot(i)
        return new(x * (1 - t) + y * t, peer, own, lambda s: w4.at[t, i // 2, s], 40)

    def p_ring(r, head):
        i = lax.rem(zh + r + 4, 4)
        buf = px if head else py
        me = y if head else x
        own = pages_ref.at[head] if r == 0 else buf.at[i, me]
        return new(me, peer_y if head else peer_x, own, lambda s: buf.at[i, s], 64)

    zw = new(zh, peer_z, w_ref, w_slot, 40)
    zp = [new(zh, peer_z, pages_ref.at[h], (lambda i: px.at[i, y]) if h else (lambda i: py.at[i, x]), 64)
          for h in (0, 1)]
    local = [
        pltpu.make_async_copy(w_ref, w_slot(zh), lsem.at[0]),
        pltpu.make_async_copy(pages_ref.at[0], py.at[zh, x], lsem.at[1]),
        pltpu.make_async_copy(pages_ref.at[1], px.at[zh, y], lsem.at[2]),
        pltpu.make_async_copy(q_ref.at[0], qy.at[y], lsem.at[3]),
        pltpu.make_async_copy(q_ref.at[1], qx.at[x], lsem.at[4]),
        pltpu.make_async_copy(rows_ref, rows_all.at[tp], lsem.at[5]),
    ]
    b = base[0]
    base[0] += 3
    r_across = remote(rows_ref, rows_all.at[tp], sems, b, across)
    r_partner = remote(rows_ref, rows_all.at[tp], sems, b + 1, partner)
    r_across.start()
    r_partner.start()
    zp[0].start()
    zp[1].start()
    zw.start()
    q_rings = [new(y, peer_y, q_ref.at[0], lambda s: qy.at[s], 64),
               new(x, peer_x, q_ref.at[1], lambda s: qx.at[s], 64)]
    p_own = [p_ring(0, 0), p_ring(0, 1)]
    w_own = w_ring(0)
    rings = [zw] + zp + q_rings + p_own + [w_own]
    for r in p_own + [w_own] + q_rings:
        r.start()
    for d in local:
        d.start()
    there = rows_all.at[2 * (1 - zl) + c]
    remote(there, there, sems, b, across).wait_recv()
    r_pass = remote(there, there, sems, b + 2, partner)
    r_pass.start()

    def step(ring):
        for r in (-1, 1):
            ring.arrived(r)
            ring.forward(r)

    late = []
    for r in (-1, 1):
        for h in (0, 1):
            zp[h].arrived(r)
            zp[h].forward(r)
            ring = p_ring(r, h)
            ring.start()
            late.append(ring)
    for r in p_own:
        step(r)
    for r in (-1, 1):
        zw.arrived(r)
        zw.forward(r)
        ring = w_ring(r)
        ring.start()
        late.append(ring)
    step(w_own)
    for r in q_rings:
        step(r)
    for h in (0, 1):
        zp[h].far()
        ring = p_ring(2, h)
        ring.start()
        late.append(ring)
    for r in late[:4]:
        step(r)
    zw.far()
    ring = w_ring(2)
    ring.start()
    late.append(ring)
    for r in late[4:6]:
        step(r)
    for r in late[6:]:
        step(r)
    for r in q_rings + p_own + [w_own] + late:
        r.far()
    mine = rows_all.at[2 * zl + 1 - c]
    remote(mine, mine, sems, b + 1, partner).wait_recv()
    other = rows_all.at[2 * (1 - zl) + 1 - c]
    remote(other, other, sems, b + 2, partner).wait_recv()
    for r in rings + late:
        r.drain()
    for d in (r_across, r_partner, r_pass):
        d.wait_send()
    for d in local:
        d.wait()
    assert base[0] <= NSEM, base[0]


NSEM = 96


def gather(rows, pages, q, w):
    s = jax.ShapeDtypeStruct
    vm = pl.BlockSpec(memory_space=pltpu.VMEM)
    return pl.pallas_call(
        gather_kernel,
        out_shape=(s((4, 32, 5120), BF), s((4, 4, 128, 256), BF), s((4, 4, 128, 256), BF),
                   s((4, 128, 640), BF), s((4, 128, 640), BF), s((2, 2, 4, 80, 1280), BF)),
        in_specs=[vm] * 4,
        out_specs=[pl.BlockSpec(memory_space=pl.ANY)] * 6,
        scratch_shapes=[pltpu.SemaphoreType.DMA((2, NSEM)), pltpu.SemaphoreType.DMA((6,))],
        compiler_params=pltpu.CompilerParams(collective_id=0, has_side_effects=True),
        name="gather",
    )(rows, pages, q, w)


F32 = jnp.float32
NT = (((1,), (1,)), ((), ()))
TN = (((0,), (0,)), ((), ()))


def attend_kernel(codes, lens, kvp_ref, qy_ref, qx_ref, py_ref, px_ref, trig_ref, reqtrig_ref,
                  o_ref, st_ref, kv_ref, q_s, m_s, l_s, acc_s):
    y, zh, x, zl, c = coords()
    me = y * 16 + zh * 4 + x
    scale = LOG2E * 128 ** -0.5
    lane = lax.broadcasted_iota(jnp.int32, (1, 128), 1)
    sign = jnp.where(lane < 64, -1.0, 1.0).astype(F32)

    def trig(r):
        cl = reqtrig_ref[0, pl.ds(r, 1), :]
        sl = reqtrig_ref[1, pl.ds(r, 1), :]
        ct, st = trig_ref[0], trig_ref[1]
        return cl * ct - sl * st, (sl * ct + cl * st) * sign

    def rope(v, cs):
        return v * cs[0] + pltpu.roll(v, 64, 1) * cs[1]

    cs_own = trig(me)
    for h in range(2):
        kv_ref[:, h * 128:(h + 1) * 128] = rope(kvp_ref[0, :, h * 128:(h + 1) * 128], cs_own).astype(BF)
    kv_ref[:, 256:512] = kvp_ref[1].astype(BF)

    row = lax.broadcasted_iota(jnp.int32, (128, 640), 0)
    col = lax.broadcasted_iota(jnp.int32, (128, 640), 1)

    def update(key, value, keep):
        s = lax.dot_general(key, q_s[...], NT, preferred_element_type=F32) * scale
        s = jnp.where(keep, s, LOW)
        m_old = m_s[0:1, :]
        m_new = jnp.maximum(m_old, jnp.max(s, axis=0, keepdims=True))
        p = jnp.exp2(s - m_new)
        a = jnp.exp2(m_old - m_new)
        l_s[0:1, :] = l_s[0:1, :] * a + jnp.sum(p, axis=0, keepdims=True)
        m_s[0:1, :] = m_new
        acc_s[...] = acc_s[...] * a + lax.dot_general(value, p.astype(BF), TN, preferred_element_type=F32)

    for t in range(2):
        q_ref, p_ref = (qy_ref, py_ref) if t == 0 else (qx_ref, px_ref)
        mine = y if t == 0 else x

        def request_of(i, t=t):
            return i * 16 + zh * 4 + x if t == 0 else y * 16 + zh * 4 + i

        def page_of(s, t=t):
            return y * 16 + s if t == 0 else (s % 4) * 16 + (s // 4) * 4 + x

        def one(i, _, t=t, q_ref=q_ref, p_ref=p_ref, mine=mine, request_of=request_of, page_of=page_of):
            r = request_of(i)

            def count(s, n):
                code = codes[page_of(s)]
                return n + jnp.where((code // 256 == r) & (code % 256 > 0), 1, 0)

            pages = lax.fori_loop(0, 16, count, jnp.int32(0))
            active = (pages > 0) | (i == mine)
            m_s[...] = jnp.full_like(m_s, LOW)
            l_s[...] = jnp.zeros_like(l_s)

            @pl.when(active)
            def _():
                cs = trig(r)
                acc_s[...] = jnp.zeros_like(acc_s)
                for h in range(5):
                    v = q_ref[i, :, h * 128:(h + 1) * 128].astype(F32)
                    q_s[h * 128:(h + 1) * 128, :] = rope(v, cs).astype(BF)

                @pl.when(i == mine)
                def _():
                    update(kv_ref[:, t * 128:(t + 1) * 128], kv_ref[:, 256 + t * 128:384 + t * 128],
                           row <= col % 128)

                def visit(s, z):
                    code = codes[page_of(s)]
                    seen = code % 256

                    @pl.when((code // 256 == r) & (seen > 0))
                    def _():
                        update(p_ref[s, :, 0:128], p_ref[s, :, 128:256], row < seen)

                    return z

                lax.fori_loop(0, 16, visit, 0)
                o_ref[t, i] = (acc_s[...] / l_s[0:1, :]).astype(BF)

            @pl.when(jnp.logical_not(active))
            def _():
                o_ref[t, i] = jnp.zeros((128, 640), BF)

            st_ref[t, i, 0:1, :] = m_s[0:1, :]
            st_ref[t, i, 1:2, :] = l_s[0:1, :]
            return 0

        lax.fori_loop(0, 4, one, 0)


def attend(codes, lens, kvp, qy, qx, py, px, trig, reqtrig):
    s = jax.ShapeDtypeStruct
    vm = pl.BlockSpec(memory_space=pltpu.VMEM)
    sm = pl.BlockSpec(memory_space=pltpu.SMEM)
    return pl.pallas_call(
        attend_kernel,
        out_shape=(s((2, 4, 128, 640), BF), s((2, 4, 8, 640), F32), s((128, 512), BF)),
        in_specs=[sm, sm] + [vm] * 7,
        out_specs=[vm] * 3,
        scratch_shapes=[pltpu.VMEM((640, 128), BF), pltpu.VMEM((8, 640), F32), pltpu.VMEM((8, 640), F32),
                        pltpu.VMEM((128, 640), F32)],
        name="attend",
    )(codes, lens, kvp, qy, qx, py.reshape(16, 128, 256), px.reshape(16, 128, 256), trig, reqtrig)


def project_kernel(o_ref, st_ref, w4_ref, fin, wv, ro, rst, relay, att, ay, ax, part, rc, ps, ra, tot, sems, wsem):
    y, zh, x, zl, c = coords()
    partner = (y, zh, x, zl, 1 - c)
    across = (y, zh, x, 1 - zl, c)
    near = [shifted(a, b) for a in (0, 2) for b in (1, -1, 2)] + [partner, across]
    load = [pltpu.make_async_copy(w4_ref.at[t], wv.at[t], wsem.at[t]) for t in range(2)]
    for d in load:
        d.start()
    barrier = pltpu.get_barrier_semaphore()
    for d in near:
        pl.semaphore_signal(barrier, inc=1, device_id=d, device_id_type=MESH)
    pl.semaphore_wait(barrier, len(near))

    axes = (0, 2)
    mine = (y, x)
    sent = []
    base = [0]

    def send(src, dst, n, device):
        d = remote(src, dst, sems, n, device)
        d.start()
        sent.append(d)

    def got(dst, n):
        remote(dst, dst, sems, n, partner).wait_recv()

    def take(n):
        base[0] += n
        return base[0] - n

    slot = lambda t, r: lax.rem(mine[t] + r + 4, 4)
    d0 = [take(9), take(9)]
    for t in range(2):
        far = o_ref.at[t, slot(t, 2)]
        for h, by in ((0, 1), (1, -1)):
            send(far.at[pl.ds(h * 64, 64)], relay.at[t, h], d0[t] + h, shifted(axes[t], by))
    for t in range(2):
        for h, by in ((0, 1), (1, -1)):
            send(st_ref.at[t, slot(t, by)], rst.at[t, h], d0[t] + 2 + h, shifted(axes[t], by))
        send(st_ref.at[t, slot(t, 2)], rst.at[t, 2], d0[t] + 4, shifted(axes[t], 2))
        for h, by in ((0, 1), (1, -1)):
            send(o_ref.at[t, slot(t, by)], ro.at[t, h], d0[t] + 5 + h, shifted(axes[t], by))
    for t in range(2):
        for h, by in ((0, 1), (1, -1)):
            got(relay.at[t, h], d0[t] + h)
            send(relay.at[t, h], ro.at[t, 2, pl.ds(h * 64, 64)], d0[t] + 7 + h, shifted(axes[t], by))
    for t in range(2):
        for h in (0, 1):
            got(rst.at[t, h], d0[t] + 2 + h)
            got(ro.at[t, h], d0[t] + 5 + h)
            got(ro.at[t, 2, pl.ds(h * 64, 64)], d0[t] + 7 + h)
        got(rst.at[t, 2], d0[t] + 4)
    for t in range(2):
        own = slot(t, 0)
        ms = [st_ref[t, own, 0:1, :]] + [rst[t, i, 0:1, :] for i in range(3)]
        ls = [st_ref[t, own, 1:2, :]] + [rst[t, i, 1:2, :] for i in range(3)]
        top = jnp.maximum(jnp.maximum(ms[0], ms[1]), jnp.maximum(ms[2], ms[3]))
        es = [jnp.exp2(m - top) * l for m, l in zip(ms, ls)]
        inv = 1.0 / (es[0] + es[1] + es[2] + es[3])
        mixed = o_ref[t, own].astype(F32) * (es[0] * inv)
        for i in range(3):
            mixed = mixed + ro[t, i].astype(F32) * (es[i + 1] * inv)
        for h in range(5):
            att[:, (t * 5 + h) * 128:(t * 5 + h + 1) * 128] = mixed[:, h * 128:(h + 1) * 128].T.astype(BF)

    bufs = (ay, ax)
    rings = []
    for t in range(2):
        rings.append(Ring(mine[t], functools.partial(shifted, axes[t]), att, (lambda s, t=t: bufs[t].at[s]), 64,
                          sems, take(4)))
        rings[t].start()
    for d in load:
        d.wait()
    g1, g2, g3 = take(8), take(8), take(8)
    order = (0, -1, 1, 2)

    def multiply(k):
        for t in range(2):
            s = slot(t, order[k])
            a = att[...] if k == 0 else bufs[t][s]
            res = lax.dot_general(a, wv[t].reshape(640, 1280), NT, preferred_element_type=F32).astype(BF)
            for z in range(2):
                for cc in range(2):
                    n = 2 * z + cc
                    part[t, k, cc, z] = res[32 * n:32 * n + 32, :]
            send(part.at[t, k, 1 - c], rc.at[t, k], g1 + 2 * k + t, partner)

    def pair(k):
        for t in range(2):
            got(rc.at[t, k], g1 + 2 * k + t)
            v = part[t, k, c, 1 - zl].astype(F32) + rc[t, k, 1 - zl].astype(F32)
            ps[t, k] = v.astype(BF)
            send(ps.at[t, k], ra.at[t, k], g2 + 2 * k + t, across)

    def finish(k):
        for t in range(2):
            got(ra.at[t, k], g2 + 2 * k + t)
            v = part[t, k, c, zl].astype(F32) + rc[t, k, zl].astype(F32) + ra[t, k].astype(F32)
            if k == 0:
                fin[t, mine[t]] = v.astype(BF)
            else:
                tot[t, k] = v.astype(BF)
                send(tot.at[t, k], fin.at[t, mine[t]], g3 + 2 * k + t, shifted(axes[t], order[k]))

    multiply(0)
    for r in (-1, 1):
        for ring in rings:
            ring.arrived(r)
            ring.forward(r)
    pair(0)
    multiply(1)
    pair(1)
    multiply(2)
    pair(2)
    finish(0)
    finish(1)
    for ring in rings:
        ring.far()
    multiply(3)
    finish(2)
    pair(3)
    finish(3)
    for t in range(2):
        for k in (1, 2, 3):
            got(fin.at[t, slot(t, -order[k])], g3 + 2 * k + t)
    for d in sent:
        d.wait_send()
    for ring in rings:
        ring.drain()
    assert base[0] <= NSEM3, base[0]


NSEM3 = 56


def project(o, st, w4):
    s = jax.ShapeDtypeStruct
    vm = pl.BlockSpec(memory_space=pltpu.VMEM)
    return pl.pallas_call(
        project_kernel,
        out_shape=s((2, 4, 32, 640), BF),
        in_specs=[vm, vm, pl.BlockSpec(memory_space=pl.ANY)],
        out_specs=vm,
        scratch_shapes=[
            pltpu.VMEM((2, 2, 4, 80, 1280), BF), pltpu.VMEM((2, 3, 128, 640), BF), pltpu.VMEM((2, 3, 8, 640), F32),
            pltpu.VMEM((2, 2, 64, 640), BF), pltpu.VMEM((128, 1280), BF), pltpu.VMEM((4, 128, 1280), BF),
            pltpu.VMEM((4, 128, 1280), BF), pltpu.VMEM((2, 4, 2, 2, 32, 640), BF), pltpu.VMEM((2, 4, 2, 32, 640), BF),
            pltpu.VMEM((2, 4, 32, 640), BF), pltpu.VMEM((2, 4, 32, 640), BF), pltpu.VMEM((2, 4, 32, 640), BF),
            pltpu.SemaphoreType.DMA((2, NSEM3)), pltpu.SemaphoreType.DMA((2,))],
        compiler_params=pltpu.CompilerParams(collective_id=1, has_side_effects=True),
        name="project",
    )(o, st, w4)


def page_codes(cached_len, page_table):
    requests, slots = page_table.shape
    r = lax.broadcasted_iota(jnp.int32, (requests, slots), 0)
    j = lax.broadcasted_iota(jnp.int32, (requests, slots), 1)
    seen = jnp.clip(cached_len[:, None] - j * 128, 0, 128)
    value = jnp.where(seen > 0, r * 256 + seen, 0)
    pages = lax.broadcasted_iota(jnp.int32, (64, 1, 1), 0)
    return jnp.sum(jnp.where(page_table[None] == pages, value[None], 0), axis=(1, 2))


def local(hidden_in, norm_gain, kv_weight, kv_bias, queries, cache_pages, out_weight, cached_len, page_table):
    pages = cache_pages[0].transpose(2, 0, 1, 3).reshape(2, 128, 256)
    q = queries.reshape(128, 2, 640).transpose(1, 0, 2)
    rows_all, py, px, qy, qx, w4 = gather(hidden_in, pages, q, out_weight.T)
    codes = page_codes(cached_len, page_table)
    inverse = jnp.power(THETA, -jnp.arange(64, dtype=F32) * 2.0 / 128)
    inverse = jnp.concatenate([inverse, inverse])

    def trig(positions):
        angles = positions.astype(F32)[:, None] * inverse[None, :]
        return jnp.stack([jnp.cos(angles), jnp.sin(angles)])

    hidden_f = rows_all.reshape(128, 5120).astype(F32)
    inverse_rms = lax.rsqrt(jnp.mean(hidden_f * hidden_f, axis=-1, keepdims=True) + EPS)
    normed = (hidden_f * inverse_rms * norm_gain.astype(F32)).astype(BF)
    kvp = jnp.einsum("td,dsc->stc", normed, kv_weight, preferred_element_type=F32)
    kvp = kvp + kv_bias.astype(F32)[:, None, :]
    o, st, kv = attend(codes, cached_len, kvp, qy, qx, py, px, trig(jnp.arange(128)), trig(cached_len))
    fin = project(o, st, w4)
    a = fin[0].reshape(4, 32, 2, 320)
    b = fin[1].reshape(4, 32, 2, 4, 80).transpose(3, 1, 2, 0, 4).reshape(4, 32, 2, 320)
    summed = jnp.stack([a, b], axis=3).transpose(1, 0, 2, 3, 4).reshape(32, 5120)
    hidden_out = (hidden_in.astype(F32) + summed.astype(F32)).astype(BF)
    return hidden_out, kv.reshape(128, 2, 2, 128)


def solution(mesh):
    fine = Mesh(mesh.devices.reshape(4, 4, 4, 2, 2), ("y", "zh", "x", "zl", "c"))
    blk, tp = ("y", "zh", "x"), ("zl", "c")
    in_specs = (P(blk + tp, None), P(), P(None, None, tp), P(None, tp), P(blk, tp),
                P(blk, None, None, tp, None), P(tp, blk), P(), P())
    out_specs = (P(blk + tp, None), P(blk, None, tp, None))
    return jax.shard_map(local, mesh=fine, in_specs=in_specs, out_specs=out_specs, check_vma=False)
```

```python
import functools

import jax
import jax.numpy as jnp
from jax import lax
from jax.experimental import pallas as pl
from jax.experimental.pallas import tpu as pltpu
from jax.sharding import Mesh, PartitionSpec as P

EPS = 1e-06
THETA = 1000000.0
LOW = -1e30
LOG2E = 1.4426950408889634
MESH = pl.DeviceIdType.MESH
HBM = pl.ANY
BF = jnp.bfloat16
F32 = jnp.float32


def coords():
    return tuple(lax.axis_index(a) for a in ("y", "zh", "x", "zl", "c"))


def shifted(axis, by):
    me = list(coords())
    me[axis] = lax.rem(me[axis] + by + 4, 4)
    return tuple(me)


def remote(src, dst, sems, n, device):
    return pltpu.make_async_remote_copy(
        src_ref=src, dst_ref=dst, send_sem=sems.at[0, n], recv_sem=sems.at[1, n],
        device_id=device, device_id_type=MESH)


class Ring:
    def __init__(self, me, peer, own, at, half, sems, base):
        self.me, self.peer, self.own, self.at, self.half = me, peer, own, at, half
        self.sems, self.base = sems, base
        self.sent = []

    def slot(self, r):
        return lax.rem(self.me + r + 4, 4)

    def part(self, s, h):
        return self.at(s).at[pl.ds(h * self.half, self.half)]

    def start(self):
        for n, by in ((0, 1), (1, -1)):
            d = remote(self.own, self.at(self.me), self.sems, self.base + n, self.peer(by))
            d.start()
            self.sent.append(d)

    def arrived(self, r):
        n = 0 if r == -1 else 1
        s = self.at(self.slot(r))
        remote(s, s, self.sems, self.base + n, self.peer(1)).wait_recv()

    def forward(self, r):
        h = 0 if r == -1 else 1
        s = self.part(self.slot(r), h)
        d = remote(s, s, self.sems, self.base + 2 + h, self.peer(-r))
        d.start()
        self.sent.append(d)

    def far(self):
        for h in (0, 1):
            s = self.part(self.slot(2), h)
            remote(s, s, self.sems, self.base + 2 + h, self.peer(1)).wait_recv()

    def drain(self):
        for d in self.sent:
            d.wait_send()


def gather_kernel(rows_ref, pages_ref, q_ref, w_ref, gain_ref, normed, py, px, qy, qx, w4, rows_all, sems, lsem):
    y, zh, x, zl, c = coords()
    partner = (y, zh, x, zl, 1 - c)
    across = (y, zh, x, 1 - zl, c)
    barrier = pltpu.get_barrier_semaphore()
    near = [shifted(a, b) for a in (0, 1, 2) for b in (1, -1)] + [partner, across]
    for d in near:
        pl.semaphore_signal(barrier, inc=1, device_id=d, device_id_type=MESH)
    pl.semaphore_wait(barrier, len(near))

    tp = 2 * zl + c
    base = [0]

    def new(me, peer, own, at, half, count=4):
        r = Ring(me, peer, own, at, half, sems, base[0])
        base[0] += count
        return r

    peer_z = lambda by: shifted(1, by)
    peer_y = lambda by: shifted(0, by)
    peer_x = lambda by: shifted(2, by)

    def w_slot(i):
        t = lax.rem(i, 2)
        return w4.at[t, i // 2, x * (1 - t) + y * t]

    def w_ring(r):
        i = lax.rem(zh + r + 4, 4)
        t = lax.rem(i, 2)
        def peer(by):
            return (lax.rem(y + t * by + 4, 4), zh, lax.rem(x + (1 - t) * by + 4, 4), zl, c)
        own = w_ref if r == 0 else w_slot(i)
        return new(x * (1 - t) + y * t, peer, own, lambda s: w4.at[t, i // 2, s], 40)

    def p_ring(r, head):
        i = lax.rem(zh + r + 4, 4)
        buf = px if head else py
        me = y if head else x
        own = pages_ref.at[head] if r == 0 else buf.at[i, me]
        return new(me, peer_y if head else peer_x, own, lambda s: buf.at[i, s], 128)

    zw = new(zh, peer_z, w_ref, w_slot, 40)
    zp = [new(zh, peer_z, pages_ref.at[h], (lambda i: px.at[i, y]) if h else (lambda i: py.at[i, x]), 128)
          for h in (0, 1)]
    def q_part(t):
        return q_ref.at[:, pl.ds(t * 640, 640)]

    def norm(block, slot):
        v = block.astype(F32)
        inverse_rms = lax.rsqrt(jnp.mean(v * v, axis=-1, keepdims=True) + EPS)
        normed[slot] = (v * inverse_rms * gain_ref[...].astype(F32)).astype(BF)

    local = [
        pltpu.make_async_copy(w_ref, w_slot(zh), lsem.at[0]),
        pltpu.make_async_copy(pages_ref.at[0], py.at[zh, x], lsem.at[1]),
        pltpu.make_async_copy(pages_ref.at[1], px.at[zh, y], lsem.at[2]),
        pltpu.make_async_copy(q_part(0), qy.at[y], lsem.at[3]),
        pltpu.make_async_copy(q_part(1), qx.at[x], lsem.at[4]),
    ]
    b = base[0]
    base[0] += 3
    r_across = remote(rows_ref, rows_all.at[tp], sems, b, across)
    r_partner = remote(rows_ref, rows_all.at[tp], sems, b + 1, partner)
    r_across.start()
    r_partner.start()
    zp[0].start()
    zp[1].start()
    zw.start()
    q_rings = [new(y, peer_y, q_part(0), lambda s: qy.at[s], 64),
               new(x, peer_x, q_part(1), lambda s: qx.at[s], 64)]
    p_own = [p_ring(0, 0), p_ring(0, 1)]
    w_own = w_ring(0)
    rings = [zw] + zp + q_rings + p_own + [w_own]
    for r in p_own + [w_own] + q_rings:
        r.start()
    for d in local:
        d.start()
    norm(rows_ref[...], tp)
    there = rows_all.at[2 * (1 - zl) + c]
    remote(there, there, sems, b, across).wait_recv()
    r_pass = remote(there, there, sems, b + 2, partner)
    r_pass.start()

    def step(ring):
        for r in (-1, 1):
            ring.arrived(r)
            ring.forward(r)

    late = []
    for r in (-1, 1):
        for h in (0, 1):
            zp[h].arrived(r)
            zp[h].forward(r)
            ring = p_ring(r, h)
            ring.start()
            late.append(ring)
    for r in p_own:
        step(r)
    for r in (-1, 1):
        zw.arrived(r)
        zw.forward(r)
        ring = w_ring(r)
        ring.start()
        late.append(ring)
    step(w_own)
    for r in q_rings:
        step(r)
    for h in (0, 1):
        zp[h].far()
        ring = p_ring(2, h)
        ring.start()
        late.append(ring)
    for r in late[:4]:
        step(r)
    zw.far()
    ring = w_ring(2)
    ring.start()
    late.append(ring)
    for r in late[4:6]:
        step(r)
    for r in late[6:]:
        step(r)
    norm(there[...], 2 * (1 - zl) + c)
    mine = rows_all.at[2 * zl + 1 - c]
    remote(mine, mine, sems, b + 1, partner).wait_recv()
    norm(mine[...], 2 * zl + 1 - c)
    other = rows_all.at[2 * (1 - zl) + 1 - c]
    remote(other, other, sems, b + 2, partner).wait_recv()
    norm(other[...], 2 * (1 - zl) + 1 - c)
    for r in q_rings + p_own + [w_own] + late:
        r.far()
    for r in rings + late:
        r.drain()
    for d in (r_across, r_partner, r_pass):
        d.wait_send()
    for d in local:
        d.wait()
    assert base[0] <= NSEM, base[0]


NSEM = 96


def gather(rows, pages, q, w, gain):
    s = jax.ShapeDtypeStruct
    vm = pl.BlockSpec(memory_space=pltpu.VMEM)
    return pl.pallas_call(
        gather_kernel,
        out_shape=(s((4, 32, 5120), BF), s((4, 4, 256, 128), BF), s((4, 4, 256, 128), BF),
                   s((4, 128, 640), BF), s((4, 128, 640), BF), s((2, 2, 4, 80, 1280), BF)),
        in_specs=[vm] * 5,
        out_specs=[vm] + [pl.BlockSpec(memory_space=pl.ANY)] * 5,
        scratch_shapes=[pltpu.VMEM((4, 32, 5120), BF), pltpu.SemaphoreType.DMA((2, NSEM)),
                        pltpu.SemaphoreType.DMA((5,))],
        compiler_params=pltpu.CompilerParams(collective_id=0, has_side_effects=True),
        name="gather",
    )(rows, pages, q, w, gain)


NT = (((1,), (1,)), ((), ()))
TN = (((0,), (0,)), ((), ()))


def attend_kernel(codes, kvp_ref, qy_ref, qx_ref, py_ref, px_ref, cos_ref, sin_ref,
                  o_ref, st_ref, kv_ref, q_s, m_s, l_s, acc_s):
    y, zh, x, zl, c = coords()
    me = y * 16 + zh * 4 + x
    scale = LOG2E * 128 ** -0.5
    lane = lax.broadcasted_iota(jnp.int32, (1, 128), 1)
    sign = jnp.where(lane < 64, -1.0, 1.0).astype(F32)

    def trig(r):
        cl = cos_ref[pl.ds(128 + r, 1), :]
        sl = sin_ref[pl.ds(128 + r, 1), :]
        ct, st = cos_ref[0:128, :], sin_ref[0:128, :]
        return cl * ct - sl * st, (sl * ct + cl * st) * sign

    def rope(v, cs):
        return v * cs[0] + pltpu.roll(v, 64, 1) * cs[1]

    cs_own = trig(me)
    for h in range(2):
        kv_ref[:, h * 128:(h + 1) * 128] = rope(kvp_ref[0, :, h * 128:(h + 1) * 128], cs_own).astype(BF)
    kv_ref[:, 256:512] = kvp_ref[1].astype(BF)

    row = lax.broadcasted_iota(jnp.int32, (128, 640), 0)
    col = lax.broadcasted_iota(jnp.int32, (128, 640), 1)

    def update(key, value, keep):
        s = lax.dot_general(key, q_s[...], NT, preferred_element_type=F32) * scale
        s = jnp.where(keep, s, LOW)
        m_old = m_s[0:1, :]
        m_new = jnp.maximum(m_old, jnp.max(s, axis=0, keepdims=True))
        p = jnp.exp2(s - m_new)
        a = jnp.exp2(m_old - m_new)
        l_s[0:1, :] = l_s[0:1, :] * a + jnp.sum(p, axis=0, keepdims=True)
        m_s[0:1, :] = m_new
        acc_s[...] = acc_s[...] * a + lax.dot_general(value, p.astype(BF), TN, preferred_element_type=F32)

    for t in range(2):
        q_ref, p_ref = (qy_ref, py_ref) if t == 0 else (qx_ref, px_ref)
        mine = y if t == 0 else x

        def request_of(i, t=t):
            return i * 16 + zh * 4 + x if t == 0 else y * 16 + zh * 4 + i

        def page_of(s, t=t):
            return y * 16 + s if t == 0 else (s % 4) * 16 + (s // 4) * 4 + x

        def one(i, _, t=t, q_ref=q_ref, p_ref=p_ref, mine=mine, request_of=request_of, page_of=page_of):
            r = request_of(i)

            def count(s, n):
                code = codes[page_of(s)]
                return n + jnp.where((code // 256 == r) & (code % 256 > 0), 1, 0)

            pages = lax.fori_loop(0, 16, count, jnp.int32(0))
            active = (pages > 0) | (i == mine)
            m_s[...] = jnp.full_like(m_s, LOW)
            l_s[...] = jnp.zeros_like(l_s)

            @pl.when(active)
            def _():
                cs = trig(r)
                acc_s[...] = jnp.zeros_like(acc_s)
                for h in range(5):
                    v = q_ref[i, :, h * 128:(h + 1) * 128].astype(F32)
                    q_s[h * 128:(h + 1) * 128, :] = rope(v, cs).astype(BF)

                @pl.when(i == mine)
                def _():
                    update(kv_ref[:, t * 128:(t + 1) * 128], kv_ref[:, 256 + t * 128:384 + t * 128],
                           row <= col % 128)

                def visit(s, z):
                    code = codes[page_of(s)]
                    seen = code % 256

                    @pl.when((code // 256 == r) & (seen > 0))
                    def _():
                        update(p_ref[s, 0:128, :], p_ref[s, 128:256, :], row < seen)

                    return z

                lax.fori_loop(0, 16, visit, 0)
                o_ref[t, i] = (acc_s[...] / l_s[0:1, :]).astype(BF)

            @pl.when(jnp.logical_not(active))
            def _():
                o_ref[t, i] = jnp.zeros((128, 640), BF)

            st_ref[t, i, 0:1, :] = m_s[0:1, :]
            st_ref[t, i, 1:2, :] = l_s[0:1, :]
            return 0

        lax.fori_loop(0, 4, one, 0)


def attend(codes, kvp, qy, qx, py, px, cos, sin):
    s = jax.ShapeDtypeStruct
    vm = pl.BlockSpec(memory_space=pltpu.VMEM)
    sm = pl.BlockSpec(memory_space=pltpu.SMEM)
    return pl.pallas_call(
        attend_kernel,
        out_shape=(s((2, 4, 128, 640), BF), s((2, 4, 8, 640), F32), s((128, 512), BF)),
        in_specs=[sm] + [vm] * 7,
        out_specs=[vm] * 3,
        scratch_shapes=[pltpu.VMEM((640, 128), BF), pltpu.VMEM((8, 640), F32), pltpu.VMEM((8, 640), F32),
                        pltpu.VMEM((128, 640), F32)],
        name="attend",
    )(codes, kvp, qy, qx, py.reshape(16, 256, 128), px.reshape(16, 256, 128), cos, sin)


def project_kernel(o_ref, st_ref, w4_ref, hid_ref, out_ref, fin, wv, ro, rst, relay, att, ay, ax, part, rc, ps, ra, tot, sems, wsem):
    y, zh, x, zl, c = coords()
    partner = (y, zh, x, zl, 1 - c)
    across = (y, zh, x, 1 - zl, c)
    near = [shifted(a, b) for a in (0, 2) for b in (1, -1, 2)] + [partner, across]
    load = [pltpu.make_async_copy(w4_ref.at[t], wv.at[t], wsem.at[t]) for t in range(2)]
    for d in load:
        d.start()
    barrier = pltpu.get_barrier_semaphore()
    for d in near:
        pl.semaphore_signal(barrier, inc=1, device_id=d, device_id_type=MESH)
    pl.semaphore_wait(barrier, len(near))

    axes = (0, 2)
    mine = (y, x)
    sent = []
    base = [0]

    def send(src, dst, n, device):
        d = remote(src, dst, sems, n, device)
        d.start()
        sent.append(d)

    def got(dst, n):
        remote(dst, dst, sems, n, partner).wait_recv()

    def take(n):
        base[0] += n
        return base[0] - n

    slot = lambda t, r: lax.rem(mine[t] + r + 4, 4)
    d0 = [take(9), take(9)]
    for t in range(2):
        far = o_ref.at[t, slot(t, 2)]
        for h, by in ((0, 1), (1, -1)):
            send(far.at[pl.ds(h * 64, 64)], relay.at[t, h], d0[t] + h, shifted(axes[t], by))
    for t in range(2):
        for h, by in ((0, 1), (1, -1)):
            send(st_ref.at[t, slot(t, by)], rst.at[t, h], d0[t] + 2 + h, shifted(axes[t], by))
        send(st_ref.at[t, slot(t, 2)], rst.at[t, 2], d0[t] + 4, shifted(axes[t], 2))
        for h, by in ((0, 1), (1, -1)):
            send(o_ref.at[t, slot(t, by)], ro.at[t, h], d0[t] + 5 + h, shifted(axes[t], by))
    for t in range(2):
        for h, by in ((0, 1), (1, -1)):
            got(relay.at[t, h], d0[t] + h)
            send(relay.at[t, h], ro.at[t, 2, pl.ds(h * 64, 64)], d0[t] + 7 + h, shifted(axes[t], by))
    for t in range(2):
        for h in (0, 1):
            got(rst.at[t, h], d0[t] + 2 + h)
            got(ro.at[t, h], d0[t] + 5 + h)
            got(ro.at[t, 2, pl.ds(h * 64, 64)], d0[t] + 7 + h)
        got(rst.at[t, 2], d0[t] + 4)
    for t in range(2):
        own = slot(t, 0)
        ms = [st_ref[t, own, 0:1, :]] + [rst[t, i, 0:1, :] for i in range(3)]
        ls = [st_ref[t, own, 1:2, :]] + [rst[t, i, 1:2, :] for i in range(3)]
        top = jnp.maximum(jnp.maximum(ms[0], ms[1]), jnp.maximum(ms[2], ms[3]))
        es = [jnp.exp2(m - top) * l for m, l in zip(ms, ls)]
        inv = 1.0 / (es[0] + es[1] + es[2] + es[3])
        mixed = o_ref[t, own].astype(F32) * (es[0] * inv)
        for i in range(3):
            mixed = mixed + ro[t, i].astype(F32) * (es[i + 1] * inv)
        for h in range(5):
            att[:, (t * 5 + h) * 128:(t * 5 + h + 1) * 128] = mixed[:, h * 128:(h + 1) * 128].T.astype(BF)

    bufs = (ay, ax)
    rings = []
    for t in range(2):
        rings.append(Ring(mine[t], functools.partial(shifted, axes[t]), att, (lambda s, t=t: bufs[t].at[s]), 64,
                          sems, take(4)))
        rings[t].start()
    for d in load:
        d.wait()
    g1, g2, g3 = take(8), take(8), take(8)
    order = (0, -1, 1, 2)

    def multiply(k):
        for t in range(2):
            s = slot(t, order[k])
            a = att[...] if k == 0 else bufs[t][s]
            res = lax.dot_general(a, wv[t].reshape(640, 1280), NT, preferred_element_type=F32).astype(BF)
            for z in range(2):
                for cc in range(2):
                    n = 2 * z + cc
                    part[t, k, cc, z] = res[32 * n:32 * n + 32, :]
            send(part.at[t, k, 1 - c], rc.at[t, k], g1 + 2 * k + t, partner)

    def pair(k):
        for t in range(2):
            got(rc.at[t, k], g1 + 2 * k + t)
            v = part[t, k, c, 1 - zl].astype(F32) + rc[t, k, 1 - zl].astype(F32)
            ps[t, k] = v.astype(BF)
            send(ps.at[t, k], ra.at[t, k], g2 + 2 * k + t, across)

    def finish(k):
        for t in range(2):
            got(ra.at[t, k], g2 + 2 * k + t)
            v = part[t, k, c, zl].astype(F32) + rc[t, k, zl].astype(F32) + ra[t, k].astype(F32)
            if k == 0:
                fin[t, mine[t]] = v.astype(BF)
            else:
                tot[t, k] = v.astype(BF)
                send(tot.at[t, k], fin.at[t, mine[t]], g3 + 2 * k + t, shifted(axes[t], order[k]))

    multiply(0)
    for r in (-1, 1):
        for ring in rings:
            ring.arrived(r)
            ring.forward(r)
    pair(0)
    multiply(1)
    pair(1)
    multiply(2)
    pair(2)
    finish(0)
    finish(1)
    for ring in rings:
        ring.far()
    multiply(3)
    finish(2)
    pair(3)
    finish(3)
    for t in range(2):
        for k in (1, 2, 3):
            got(fin.at[t, slot(t, -order[k])], g3 + 2 * k + t)
    for u in range(4):
        for g in range(2):
            pieces = [fin[0, u].astype(F32)[:, g * 320:g * 320 + 320]]
            for s in range(4):
                first = g * 320 + u * 80
                pieces.append(fin[1, s].astype(F32)[:, first:first + 80])
            cols = pl.ds(u * 1280 + g * 640, 640)
            summed = jnp.concatenate(pieces, axis=1)
            out_ref[:, cols] = (hid_ref[:, cols].astype(F32) + summed).astype(BF)
    for d in sent:
        d.wait_send()
    for ring in rings:
        ring.drain()
    assert base[0] <= NSEM3, base[0]


NSEM3 = 56


def project(o, st, w4, hidden):
    s = jax.ShapeDtypeStruct
    vm = pl.BlockSpec(memory_space=pltpu.VMEM)
    return pl.pallas_call(
        project_kernel,
        out_shape=s((32, 5120), BF),
        in_specs=[vm, vm, pl.BlockSpec(memory_space=pl.ANY), vm],
        out_specs=vm,
        scratch_shapes=[
            pltpu.VMEM((2, 4, 32, 640), BF),
            pltpu.VMEM((2, 2, 4, 80, 1280), BF), pltpu.VMEM((2, 3, 128, 640), BF), pltpu.VMEM((2, 3, 8, 640), F32),
            pltpu.VMEM((2, 2, 64, 640), BF), pltpu.VMEM((128, 1280), BF), pltpu.VMEM((4, 128, 1280), BF),
            pltpu.VMEM((4, 128, 1280), BF), pltpu.VMEM((2, 4, 2, 2, 32, 640), BF), pltpu.VMEM((2, 4, 2, 32, 640), BF),
            pltpu.VMEM((2, 4, 32, 640), BF), pltpu.VMEM((2, 4, 32, 640), BF), pltpu.VMEM((2, 4, 32, 640), BF),
            pltpu.SemaphoreType.DMA((2, NSEM3)), pltpu.SemaphoreType.DMA((2,))],
        compiler_params=pltpu.CompilerParams(collective_id=1, has_side_effects=True),
        name="project",
    )(o, st, w4, hidden)


def page_codes(cached_len, page_table):
    requests, slots = page_table.shape
    r = lax.broadcasted_iota(jnp.int32, (requests, slots), 0)
    j = lax.broadcasted_iota(jnp.int32, (requests, slots), 1)
    seen = jnp.clip(cached_len[:, None] - j * 128, 0, 128)
    value = jnp.where(seen > 0, r * 256 + seen, 0).reshape(1, -1)
    pages = lax.broadcasted_iota(jnp.int32, (64, 1), 0)
    return jnp.sum(jnp.where(page_table.reshape(1, -1) == pages, value, 0), axis=1)


def local(hidden_in, norm_gain, kv_weight, kv_bias, queries, cache_pages, out_weight, cached_len, page_table):
    pages = cache_pages[0].transpose(2, 1, 0, 3).reshape(2, 256, 128)
    normed, py, px, qy, qx, w4 = gather(hidden_in, pages, queries, out_weight.T, norm_gain.reshape(1, 5120))
    codes = page_codes(cached_len, page_table)
    pair = lax.broadcasted_iota(jnp.int32, (1, 128), 1) % 64
    inverse = jnp.power(THETA, -pair.astype(F32) * 2.0 / 128)
    positions = jnp.concatenate([jnp.arange(128, dtype=jnp.int32), cached_len])
    angles = positions.astype(F32)[:, None] * inverse
    kvp = jnp.einsum("td,dsc->stc", normed.reshape(128, 5120), kv_weight, preferred_element_type=F32)
    kvp = kvp + kv_bias.astype(F32)[:, None, :]
    o, st, kv = attend(codes, kvp, qy, qx, py, px, jnp.cos(angles), jnp.sin(angles))
    return project(o, st, w4, hidden_in), kv.reshape(128, 2, 2, 128)


def solution(mesh):
    fine = Mesh(mesh.devices.reshape(4, 4, 4, 2, 2), ("y", "zh", "x", "zl", "c"))
    blk, tp = ("y", "zh", "x"), ("zl", "c")
    in_specs = (P(blk + tp, None), P(), P(None, None, tp), P(None, tp), P(blk, tp),
                P(blk, None, None, tp, None), P(tp, blk), P(), P())
    out_specs = (P(blk + tp, None), P(blk, None, tp, None))
    return jax.shard_map(local, mesh=fine, in_specs=in_specs, out_specs=out_specs, check_vma=False)
```

```python
import functools

import jax
import jax.numpy as jnp
from jax import lax
from jax.experimental import pallas as pl
from jax.experimental.pallas import tpu as pltpu
from jax.sharding import Mesh, PartitionSpec as P

EPS = 1e-06
THETA = 1000000.0
LOW = -1e30
LOG2E = 1.4426950408889634
MESH = pl.DeviceIdType.MESH
HBM = pl.ANY
BF = jnp.bfloat16
F32 = jnp.float32


def coords():
    return tuple(lax.axis_index(a) for a in ("y", "zh", "x", "zl", "c"))


def shifted(axis, by):
    me = list(coords())
    me[axis] = lax.rem(me[axis] + by + 4, 4)
    return tuple(me)


def remote(src, dst, sems, n, device):
    return pltpu.make_async_remote_copy(
        src_ref=src, dst_ref=dst, send_sem=sems.at[0, n], recv_sem=sems.at[1, n],
        device_id=device, device_id_type=MESH)


class Ring:
    def __init__(self, me, peer, own, at, half, sems, base):
        self.me, self.peer, self.own, self.at, self.half = me, peer, own, at, half
        self.sems, self.base = sems, base
        self.sent = []

    def slot(self, r):
        return lax.rem(self.me + r + 4, 4)

    def part(self, s, h):
        return self.at(s).at[pl.ds(h * self.half, self.half)]

    def start(self):
        for n, by in ((0, 1), (1, -1)):
            d = remote(self.own, self.at(self.me), self.sems, self.base + n, self.peer(by))
            d.start()
            self.sent.append(d)

    def arrived(self, r):
        n = 0 if r == -1 else 1
        s = self.at(self.slot(r))
        remote(s, s, self.sems, self.base + n, self.peer(1)).wait_recv()

    def forward(self, r):
        h = 0 if r == -1 else 1
        s = self.part(self.slot(r), h)
        d = remote(s, s, self.sems, self.base + 2 + h, self.peer(-r))
        d.start()
        self.sent.append(d)

    def far(self):
        for h in (0, 1):
            s = self.part(self.slot(2), h)
            remote(s, s, self.sems, self.base + 2 + h, self.peer(1)).wait_recv()

    def drain(self):
        for d in self.sent:
            d.wait_send()


def gather_kernel(rows_ref, pages_ref, q_ref, w_ref, gain_ref, table_ref, value_ref, normed, py, px, qy, qx, w4,
                  codes, rows_all, sems, lsem):
    y, zh, x, zl, c = coords()
    partner = (y, zh, x, zl, 1 - c)
    across = (y, zh, x, 1 - zl, c)
    barrier = pltpu.get_barrier_semaphore()
    near = [shifted(a, b) for a in (0, 1, 2) for b in (1, -1)] + [partner, across]
    for d in near:
        pl.semaphore_signal(barrier, inc=1, device_id=d, device_id_type=MESH)
    pl.semaphore_wait(barrier, len(near))

    tp = 2 * zl + c
    base = [0]

    def new(me, peer, own, at, half, count=4):
        r = Ring(me, peer, own, at, half, sems, base[0])
        base[0] += count
        return r

    peer_z = lambda by: shifted(1, by)
    peer_y = lambda by: shifted(0, by)
    peer_x = lambda by: shifted(2, by)

    def w_slot(i):
        t = lax.rem(i, 2)
        return w4.at[t, i // 2, x * (1 - t) + y * t]

    def w_ring(r):
        i = lax.rem(zh + r + 4, 4)
        t = lax.rem(i, 2)
        def peer(by):
            return (lax.rem(y + t * by + 4, 4), zh, lax.rem(x + (1 - t) * by + 4, 4), zl, c)
        own = w_ref if r == 0 else w_slot(i)
        return new(x * (1 - t) + y * t, peer, own, lambda s: w4.at[t, i // 2, s], 40)

    def p_ring(r, head):
        i = lax.rem(zh + r + 4, 4)
        buf = px if head else py
        me = y if head else x
        own = pages_ref.at[head] if r == 0 else buf.at[i, me]
        return new(me, peer_y if head else peer_x, own, lambda s: buf.at[i, s], 128)

    zw = new(zh, peer_z, w_ref, w_slot, 40)
    zp = [new(zh, peer_z, pages_ref.at[h], (lambda i: px.at[i, y]) if h else (lambda i: py.at[i, x]), 128)
          for h in (0, 1)]
    def q_part(t):
        return q_ref.at[:, pl.ds(t * 640, 640)]

    def norm(block, slot):
        v = block.astype(F32)
        inverse_rms = lax.rsqrt(jnp.mean(v * v, axis=-1, keepdims=True) + EPS)
        v = v * inverse_rms
        for k in range(40):
            cols = pl.ds(k * 128, 128)
            normed[slot, :, cols] = (v[:, k * 128:k * 128 + 128] * gain_ref[k:k + 1, :].astype(F32)).astype(BF)

    def find_codes():
        table, value = table_ref[...], value_ref[...]
        row = lax.broadcasted_iota(jnp.int32, (64, 128), 0)
        lane = lax.broadcasted_iota(jnp.int32, (64, 128), 1)
        rows = [jnp.sum(jnp.where(table == p, value, 0), axis=0, keepdims=True) for p in range(64)]
        each = jnp.sum(jnp.concatenate(rows, axis=0), axis=1, keepdims=True)
        codes[0:1, :] = jnp.sum(jnp.where(row == lane, each, 0), axis=0, keepdims=True)
        codes[1:8, :] = jnp.zeros((7, 128), jnp.int32)

    local = [
        pltpu.make_async_copy(w_ref, w_slot(zh), lsem.at[0]),
        pltpu.make_async_copy(pages_ref.at[0], py.at[zh, x], lsem.at[1]),
        pltpu.make_async_copy(pages_ref.at[1], px.at[zh, y], lsem.at[2]),
        pltpu.make_async_copy(q_part(0), qy.at[y], lsem.at[3]),
        pltpu.make_async_copy(q_part(1), qx.at[x], lsem.at[4]),
    ]
    b = base[0]
    base[0] += 3
    r_across = remote(rows_ref, rows_all.at[tp], sems, b, across)
    r_partner = remote(rows_ref, rows_all.at[tp], sems, b + 1, partner)
    zp[0].start()
    zp[1].start()
    zw.start()
    r_partner.start()
    q_rings = [new(y, peer_y, q_part(0), lambda s: qy.at[s], 64),
               new(x, peer_x, q_part(1), lambda s: qx.at[s], 64)]
    p_own = [p_ring(0, 0), p_ring(0, 1)]
    w_own = w_ring(0)
    rings = [zw] + zp + q_rings + p_own + [w_own]
    for r in p_own + [w_own] + q_rings:
        r.start()
    for d in local:
        d.start()
    norm(rows_ref[...], tp)
    there = rows_all.at[2 * (1 - zl) + c]
    mine = rows_all.at[2 * zl + 1 - c]
    other = rows_all.at[2 * (1 - zl) + 1 - c]

    def step(ring):
        for r in (-1, 1):
            ring.arrived(r)
            ring.forward(r)

    late = []

    def begin(ring):
        ring.start()
        late.append(ring)
        return ring

    for r in p_own:
        step(r)
    p_near = []
    for r in (-1, 1):
        for h in (0, 1):
            zp[h].arrived(r)
            zp[h].forward(r)
            p_near.append(begin(p_ring(r, h)))
    step(w_own)
    for r in q_rings:
        step(r)
    for r in p_near:
        step(r)
    w_near = []
    for r in (-1, 1):
        zw.arrived(r)
        zw.forward(r)
        w_near.append(begin(w_ring(r)))
    r_across.start()
    remote(mine, mine, sems, b + 1, partner).wait_recv()
    norm(mine[...], 2 * zl + 1 - c)
    find_codes()
    p_far = []
    for h in (0, 1):
        zp[h].far()
        p_far.append(begin(p_ring(2, h)))
    step(w_near[0])
    zw.far()
    w_far = begin(w_ring(2))
    step(w_near[1])
    for r in p_far:
        step(r)
    remote(there, there, sems, b, across).wait_recv()
    r_pass = remote(there, there, sems, b + 2, partner)
    r_pass.start()
    norm(there[...], 2 * (1 - zl) + c)
    step(w_far)
    remote(other, other, sems, b + 2, partner).wait_recv()
    norm(other[...], 2 * (1 - zl) + 1 - c)
    for r in q_rings + p_own + [w_own] + late:
        r.far()
    for r in rings + late:
        r.drain()
    for d in (r_across, r_partner, r_pass):
        d.wait_send()
    for d in local:
        d.wait()
    assert base[0] <= NSEM, base[0]


NSEM = 96


def gather(rows, pages, q, w, gain, table, value):
    s = jax.ShapeDtypeStruct
    vm = pl.BlockSpec(memory_space=pltpu.VMEM)
    return pl.pallas_call(
        gather_kernel,
        out_shape=(s((4, 32, 5120), BF), s((4, 4, 256, 128), BF), s((4, 4, 256, 128), BF),
                   s((4, 128, 640), BF), s((4, 128, 640), BF), s((2, 2, 4, 80, 1280), BF),
                   s((8, 128), jnp.int32)),
        in_specs=[vm] * 7,
        out_specs=[vm] + [pl.BlockSpec(memory_space=pl.ANY)] * 5 + [vm],
        scratch_shapes=[pltpu.VMEM((4, 32, 5120), BF), pltpu.SemaphoreType.DMA((2, NSEM)),
                        pltpu.SemaphoreType.DMA((5,))],
        compiler_params=pltpu.CompilerParams(collective_id=0, has_side_effects=True),
        name="gather",
    )(rows, pages, q, w, gain, table, value)


NT = (((1,), (1,)), ((), ()))
TN = (((0,), (0,)), ((), ()))


def attend_kernel(codes, kvp_ref, qy_ref, qx_ref, py_ref, px_ref, cos_ref, sin_ref, rcos_ref, rsin_ref,
                  o_ref, st_ref, kv_ref, q_s, m_s, l_s, acc_s):
    y, zh, x, zl, c = coords()
    me = y * 16 + zh * 4 + x
    scale = LOG2E * 128 ** -0.5
    lane = lax.broadcasted_iota(jnp.int32, (1, 128), 1)
    sign = jnp.where(lane < 64, -1.0, 1.0).astype(F32)

    def trig(r):
        cl = rcos_ref[pl.ds(r, 1), :]
        sl = rsin_ref[pl.ds(r, 1), :]
        ct, st = cos_ref[...], sin_ref[...]
        return cl * ct - sl * st, (sl * ct + cl * st) * sign

    def rope(v, cs):
        return v * cs[0] + pltpu.roll(v, 64, 1) * cs[1]

    cs_own = trig(me)
    for h in range(2):
        kv_ref[:, h * 128:(h + 1) * 128] = rope(kvp_ref[0, :, h * 128:(h + 1) * 128], cs_own).astype(BF)
    kv_ref[:, 256:512] = kvp_ref[1].astype(BF)

    row = lax.broadcasted_iota(jnp.int32, (128, 640), 0)
    col = lax.broadcasted_iota(jnp.int32, (128, 640), 1)

    def update(key, value, keep):
        s = lax.dot_general(key, q_s[...], NT, preferred_element_type=F32) * scale
        s = jnp.where(keep, s, LOW)
        m_old = m_s[0:1, :]
        m_new = jnp.maximum(m_old, jnp.max(s, axis=0, keepdims=True))
        p = jnp.exp2(s - m_new)
        a = jnp.exp2(m_old - m_new)
        l_s[0:1, :] = l_s[0:1, :] * a + jnp.sum(p, axis=0, keepdims=True)
        m_s[0:1, :] = m_new
        acc_s[...] = acc_s[...] * a + lax.dot_general(value, p.astype(BF), TN, preferred_element_type=F32)

    for t in range(2):
        q_ref, p_ref = (qy_ref, py_ref) if t == 0 else (qx_ref, px_ref)
        mine = y if t == 0 else x

        def request_of(i, t=t):
            return i * 16 + zh * 4 + x if t == 0 else y * 16 + zh * 4 + i

        def page_of(s, t=t):
            return y * 16 + s if t == 0 else (s % 4) * 16 + (s // 4) * 4 + x

        def one(i, _, t=t, q_ref=q_ref, p_ref=p_ref, mine=mine, request_of=request_of, page_of=page_of):
            r = request_of(i)

            def count(s, n):
                code = codes[0, page_of(s)]
                return n + jnp.where((code // 256 == r) & (code % 256 > 0), 1, 0)

            pages = lax.fori_loop(0, 16, count, jnp.int32(0))
            active = (pages > 0) | (i == mine)
            m_s[...] = jnp.full_like(m_s, LOW)
            l_s[...] = jnp.zeros_like(l_s)

            @pl.when(active)
            def _():
                cs = trig(r)
                acc_s[...] = jnp.zeros_like(acc_s)
                for h in range(5):
                    v = q_ref[i, :, h * 128:(h + 1) * 128].astype(F32)
                    q_s[h * 128:(h + 1) * 128, :] = rope(v, cs).astype(BF)

                @pl.when(i == mine)
                def _():
                    update(kv_ref[:, t * 128:(t + 1) * 128], kv_ref[:, 256 + t * 128:384 + t * 128],
                           row <= col % 128)

                def visit(s, z):
                    code = codes[0, page_of(s)]
                    seen = code % 256

                    @pl.when((code // 256 == r) & (seen > 0))
                    def _():
                        update(p_ref[s, 0:128, :], p_ref[s, 128:256, :], row < seen)

                    return z

                lax.fori_loop(0, 16, visit, 0)
                o_ref[t, i] = (acc_s[...] / l_s[0:1, :]).astype(BF)

            @pl.when(jnp.logical_not(active))
            def _():
                o_ref[t, i] = jnp.zeros((128, 640), BF)

            st_ref[t, i, 0:1, :] = m_s[0:1, :]
            st_ref[t, i, 1:2, :] = l_s[0:1, :]
            return 0

        lax.fori_loop(0, 4, one, 0)


def attend(codes, kvp, qy, qx, py, px, trigs):
    s = jax.ShapeDtypeStruct
    vm = pl.BlockSpec(memory_space=pltpu.VMEM)
    sm = pl.BlockSpec(memory_space=pltpu.SMEM)
    return pl.pallas_call(
        attend_kernel,
        out_shape=(s((2, 4, 128, 640), BF), s((2, 4, 8, 640), F32), s((128, 512), BF)),
        in_specs=[sm] + [vm] * 9,
        out_specs=[vm] * 3,
        scratch_shapes=[pltpu.VMEM((640, 128), BF), pltpu.VMEM((8, 640), F32), pltpu.VMEM((8, 640), F32),
                        pltpu.VMEM((128, 640), F32)],
        name="attend",
    )(codes, kvp, qy, qx, py.reshape(16, 256, 128), px.reshape(16, 256, 128), *trigs)


def project_kernel(o_ref, st_ref, w4_ref, hid_ref, out_ref, fin, wv, ro, rst, relay, att, ay, ax, part, rc, ps, ra, tot, sems, wsem):
    y, zh, x, zl, c = coords()
    partner = (y, zh, x, zl, 1 - c)
    across = (y, zh, x, 1 - zl, c)
    near = [shifted(a, b) for a in (0, 2) for b in (1, -1, 2)] + [partner, across]
    load = [pltpu.make_async_copy(w4_ref.at[t], wv.at[t], wsem.at[t]) for t in range(2)]
    for d in load:
        d.start()
    barrier = pltpu.get_barrier_semaphore()
    for d in near:
        pl.semaphore_signal(barrier, inc=1, device_id=d, device_id_type=MESH)
    pl.semaphore_wait(barrier, len(near))

    axes = (0, 2)
    mine = (y, x)
    sent = []
    base = [0]

    def send(src, dst, n, device):
        d = remote(src, dst, sems, n, device)
        d.start()
        sent.append(d)

    def got(dst, n):
        remote(dst, dst, sems, n, partner).wait_recv()

    def take(n):
        base[0] += n
        return base[0] - n

    slot = lambda t, r: lax.rem(mine[t] + r + 4, 4)
    d0 = [take(9), take(9)]
    for t in range(2):
        far = o_ref.at[t, slot(t, 2)]
        for h, by in ((0, 1), (1, -1)):
            send(far.at[pl.ds(h * 64, 64)], relay.at[t, h], d0[t] + h, shifted(axes[t], by))
    for t in range(2):
        for h, by in ((0, 1), (1, -1)):
            send(st_ref.at[t, slot(t, by)], rst.at[t, h], d0[t] + 2 + h, shifted(axes[t], by))
        send(st_ref.at[t, slot(t, 2)], rst.at[t, 2], d0[t] + 4, shifted(axes[t], 2))
        for h, by in ((0, 1), (1, -1)):
            send(o_ref.at[t, slot(t, by)], ro.at[t, h], d0[t] + 5 + h, shifted(axes[t], by))
    for t in range(2):
        for h, by in ((0, 1), (1, -1)):
            got(relay.at[t, h], d0[t] + h)
            send(relay.at[t, h], ro.at[t, 2, pl.ds(h * 64, 64)], d0[t] + 7 + h, shifted(axes[t], by))
    for t in range(2):
        for h in (0, 1):
            got(rst.at[t, h], d0[t] + 2 + h)
            got(ro.at[t, h], d0[t] + 5 + h)
            got(ro.at[t, 2, pl.ds(h * 64, 64)], d0[t] + 7 + h)
        got(rst.at[t, 2], d0[t] + 4)
    for t in range(2):
        own = slot(t, 0)
        ms = [st_ref[t, own, 0:1, :]] + [rst[t, i, 0:1, :] for i in range(3)]
        ls = [st_ref[t, own, 1:2, :]] + [rst[t, i, 1:2, :] for i in range(3)]
        top = jnp.maximum(jnp.maximum(ms[0], ms[1]), jnp.maximum(ms[2], ms[3]))
        es = [jnp.exp2(m - top) * l for m, l in zip(ms, ls)]
        inv = 1.0 / (es[0] + es[1] + es[2] + es[3])
        mixed = o_ref[t, own].astype(F32) * (es[0] * inv)
        for i in range(3):
            mixed = mixed + ro[t, i].astype(F32) * (es[i + 1] * inv)
        for h in range(5):
            att[:, (t * 5 + h) * 128:(t * 5 + h + 1) * 128] = mixed[:, h * 128:(h + 1) * 128].T.astype(BF)

    bufs = (ay, ax)
    rings = []
    for t in range(2):
        rings.append(Ring(mine[t], functools.partial(shifted, axes[t]), att, (lambda s, t=t: bufs[t].at[s]), 64,
                          sems, take(4)))
        rings[t].start()
    for d in load:
        d.wait()
    g1, g2, g3 = take(8), take(8), take(8)
    order = (0, -1, 1, 2)

    def multiply(k):
        for t in range(2):
            s = slot(t, order[k])
            a = att[...] if k == 0 else bufs[t][s]
            res = lax.dot_general(a, wv[t].reshape(640, 1280), NT, preferred_element_type=F32).astype(BF)
            for z in range(2):
                for cc in range(2):
                    n = 2 * z + cc
                    part[t, k, cc, z] = res[32 * n:32 * n + 32, :]
            send(part.at[t, k, 1 - c], rc.at[t, k], g1 + 2 * k + t, partner)

    def pair(k):
        for t in range(2):
            got(rc.at[t, k], g1 + 2 * k + t)
            v = part[t, k, c, 1 - zl].astype(F32) + rc[t, k, 1 - zl].astype(F32)
            ps[t, k] = v.astype(BF)
            send(ps.at[t, k], ra.at[t, k], g2 + 2 * k + t, across)

    def finish(k):
        for t in range(2):
            got(ra.at[t, k], g2 + 2 * k + t)
            v = part[t, k, c, zl].astype(F32) + rc[t, k, zl].astype(F32) + ra[t, k].astype(F32)
            if k == 0:
                fin[t, mine[t]] = v.astype(BF)
            else:
                tot[t, k] = v.astype(BF)
                send(tot.at[t, k], fin.at[t, mine[t]], g3 + 2 * k + t, shifted(axes[t], order[k]))

    multiply(0)
    for r in (-1, 1):
        for ring in rings:
            ring.arrived(r)
            ring.forward(r)
    pair(0)
    multiply(1)
    pair(1)
    multiply(2)
    pair(2)
    finish(0)
    finish(1)
    for ring in rings:
        ring.far()
    multiply(3)
    finish(2)
    pair(3)
    finish(3)
    for t in range(2):
        for k in (1, 2, 3):
            got(fin.at[t, slot(t, -order[k])], g3 + 2 * k + t)
    for u in range(4):
        for g in range(2):
            pieces = [fin[0, u].astype(F32)[:, g * 320:g * 320 + 320]]
            for s in range(4):
                first = g * 320 + u * 80
                pieces.append(fin[1, s].astype(F32)[:, first:first + 80])
            cols = pl.ds(u * 1280 + g * 640, 640)
            summed = jnp.concatenate(pieces, axis=1)
            out_ref[:, cols] = (hid_ref[:, cols].astype(F32) + summed).astype(BF)
    for d in sent:
        d.wait_send()
    for ring in rings:
        ring.drain()
    assert base[0] <= NSEM3, base[0]


NSEM3 = 56


def project(o, st, w4, hidden):
    s = jax.ShapeDtypeStruct
    vm = pl.BlockSpec(memory_space=pltpu.VMEM)
    return pl.pallas_call(
        project_kernel,
        out_shape=s((32, 5120), BF),
        in_specs=[vm, vm, pl.BlockSpec(memory_space=pl.ANY), vm],
        out_specs=vm,
        scratch_shapes=[
            pltpu.VMEM((2, 4, 32, 640), BF),
            pltpu.VMEM((2, 2, 4, 80, 1280), BF), pltpu.VMEM((2, 3, 128, 640), BF), pltpu.VMEM((2, 3, 8, 640), F32),
            pltpu.VMEM((2, 2, 64, 640), BF), pltpu.VMEM((128, 1280), BF), pltpu.VMEM((4, 128, 1280), BF),
            pltpu.VMEM((4, 128, 1280), BF), pltpu.VMEM((2, 4, 2, 2, 32, 640), BF), pltpu.VMEM((2, 4, 2, 32, 640), BF),
            pltpu.VMEM((2, 4, 32, 640), BF), pltpu.VMEM((2, 4, 32, 640), BF), pltpu.VMEM((2, 4, 32, 640), BF),
            pltpu.SemaphoreType.DMA((2, NSEM3)), pltpu.SemaphoreType.DMA((2,))],
        compiler_params=pltpu.CompilerParams(collective_id=1, has_side_effects=True),
        name="project",
    )(o, st, w4, hidden)


def entry_values(cached_len, shape):
    r = lax.broadcasted_iota(jnp.int32, shape, 0)
    j = lax.broadcasted_iota(jnp.int32, shape, 1)
    seen = jnp.clip(cached_len[:, None] - j * 128, 0, 128)
    return jnp.where(seen > 0, r * 256 + seen, 0)


def local(hidden_in, norm_gain, kv_weight, kv_bias, queries, cache_pages, out_weight, cached_len, page_table):
    pages = cache_pages[0].transpose(2, 1, 0, 3).reshape(2, 256, 128)
    normed, py, px, qy, qx, w4, codes = gather(
        hidden_in, pages, queries, out_weight.T, norm_gain.reshape(40, 128),
        page_table, entry_values(cached_len, page_table.shape))
    pair = lax.broadcasted_iota(jnp.int32, (1, 128), 1) % 64
    inverse = jnp.power(THETA, -pair.astype(F32) * 2.0 / 128)
    trigs = []
    for positions in (jnp.arange(128), cached_len):
        angles = positions.astype(F32)[:, None] * inverse
        trigs += [jnp.cos(angles), jnp.sin(angles)]
    kvp = jnp.einsum("td,dsc->stc", normed.reshape(128, 5120), kv_weight, preferred_element_type=F32)
    kvp = kvp + kv_bias.astype(F32)[:, None, :]
    o, st, kv = attend(codes, kvp, qy, qx, py, px, trigs)
    return project(o, st, w4, hidden_in), kv.reshape(128, 2, 2, 128)


def solution(mesh):
    fine = Mesh(mesh.devices.reshape(4, 4, 4, 2, 2), ("y", "zh", "x", "zl", "c"))
    blk, tp = ("y", "zh", "x"), ("zl", "c")
    in_specs = (P(blk + tp, None), P(), P(None, None, tp), P(None, tp), P(blk, tp),
                P(blk, None, None, tp, None), P(tp, blk), P(), P())
    out_specs = (P(blk + tp, None), P(blk, None, tp, None))
    return jax.shard_map(local, mesh=fine, in_specs=in_specs, out_specs=out_specs, check_vma=False)
```

```python
import functools

import jax
import jax.numpy as jnp
from jax import lax
from jax.experimental import pallas as pl
from jax.experimental.pallas import tpu as pltpu
from jax.sharding import Mesh, PartitionSpec as P

EPS = 1e-06
THETA = 1000000.0
LOW = -1e30
LOG2E = 1.4426950408889634
MESH = pl.DeviceIdType.MESH
HBM = pl.ANY
BF = jnp.bfloat16
F32 = jnp.float32


def coords():
    return tuple(lax.axis_index(a) for a in ("y", "zh", "x", "zl", "c"))


def shifted(axis, by):
    me = list(coords())
    me[axis] = lax.rem(me[axis] + by + 4, 4)
    return tuple(me)


def remote(src, dst, sems, n, device):
    return pltpu.make_async_remote_copy(
        src_ref=src, dst_ref=dst, send_sem=sems.at[0, n], recv_sem=sems.at[1, n],
        device_id=device, device_id_type=MESH)


class Ring:
    def __init__(self, me, peer, own, at, half, sems, base):
        self.me, self.peer, self.own, self.at, self.half = me, peer, own, at, half
        self.sems, self.base = sems, base
        self.sent = []

    def slot(self, r):
        return lax.rem(self.me + r + 4, 4)

    def part(self, s, h):
        return self.at(s).at[pl.ds(h * self.half, self.half)]

    def start(self):
        for second in (0, 1):
            for n, by in ((0, 1), (1, -1)):
                h = n ^ second
                src = self.own.at[pl.ds(h * self.half, self.half)]
                d = remote(src, self.part(self.me, h), self.sems, self.base + 4 * second + n, self.peer(by))
                d.start()
                self.sent.append(d)

    def landed(self, r, second):
        n = 0 if r == -1 else 1
        s = self.part(self.slot(r), n ^ second)
        remote(s, s, self.sems, self.base + 4 * second + n, self.peer(1)).wait_recv()

    def arrived(self, r):
        self.landed(r, 0)

    def rest(self, r):
        self.landed(r, 1)

    def forward(self, r):
        h = 0 if r == -1 else 1
        s = self.part(self.slot(r), h)
        d = remote(s, s, self.sems, self.base + 2 + h, self.peer(-r))
        d.start()
        self.sent.append(d)

    def far(self):
        for h in (0, 1):
            s = self.part(self.slot(2), h)
            remote(s, s, self.sems, self.base + 2 + h, self.peer(1)).wait_recv()

    def drain(self):
        for d in self.sent:
            d.wait_send()


def gather_kernel(rows_ref, pages_ref, q_ref, w_ref, gain_ref, table_ref, lens_ref, inv_ref, normed, py, px, qy, qx, w4,
                  codes, trig, rtrig, rows_all, sems, lsem):
    y, zh, x, zl, c = coords()
    partner = (y, zh, x, zl, 1 - c)
    across = (y, zh, x, 1 - zl, c)
    barrier = pltpu.get_barrier_semaphore()
    near = [shifted(a, b) for a in (0, 1, 2) for b in (1, -1)] + [partner, across]
    for d in near:
        pl.semaphore_signal(barrier, inc=1, device_id=d, device_id_type=MESH)
    pl.semaphore_wait(barrier, len(near))

    tp = 2 * zl + c
    base = [0]

    def new(me, peer, own, at, half, count=6):
        r = Ring(me, peer, own, at, half, sems, base[0])
        base[0] += count
        return r

    peer_z = lambda by: shifted(1, by)
    peer_y = lambda by: shifted(0, by)
    peer_x = lambda by: shifted(2, by)

    def w_slot(i):
        t = lax.rem(i, 2)
        return w4.at[t, i // 2, x * (1 - t) + y * t]

    def w_ring(r):
        i = lax.rem(zh + r + 4, 4)
        t = lax.rem(i, 2)
        def peer(by):
            return (lax.rem(y + t * by + 4, 4), zh, lax.rem(x + (1 - t) * by + 4, 4), zl, c)
        own = w_ref if r == 0 else w_slot(i)
        return new(x * (1 - t) + y * t, peer, own, lambda s: w4.at[t, i // 2, s], 40)

    def p_ring(r, head):
        i = lax.rem(zh + r + 4, 4)
        buf = px if head else py
        me = y if head else x
        own = pages_ref.at[head] if r == 0 else buf.at[i, me]
        return new(me, peer_y if head else peer_x, own, lambda s: buf.at[i, s], 128)

    zw = new(zh, peer_z, w_ref, w_slot, 40)
    zp = [new(zh, peer_z, pages_ref.at[h], (lambda i: px.at[i, y]) if h else (lambda i: py.at[i, x]), 128)
          for h in (0, 1)]
    def q_part(t):
        return q_ref.at[:, pl.ds(t * 640, 640)]

    def norm(block, slot):
        v = block.astype(F32)
        inverse_rms = lax.rsqrt(jnp.mean(v * v, axis=-1, keepdims=True) + EPS)
        v = v * inverse_rms
        for k in range(40):
            cols = pl.ds(k * 128, 128)
            normed[slot, :, cols] = (v[:, k * 128:k * 128 + 128] * gain_ref[k:k + 1, :].astype(F32)).astype(BF)

    def find_codes():
        table = table_ref[...]
        r = lax.broadcasted_iota(jnp.int32, (32, 64), 1)
        j = lax.broadcasted_iota(jnp.int32, (32, 64), 0)
        seen = jnp.clip(lens_ref[...] - j * 128, 0, 128)
        value = jnp.where(seen > 0, r * 256 + seen, 0)
        row = lax.broadcasted_iota(jnp.int32, (64, 128), 0)
        lane = lax.broadcasted_iota(jnp.int32, (64, 128), 1)
        rows = [jnp.sum(jnp.where(table == p, value, 0), axis=0, keepdims=True) for p in range(64)]
        each = jnp.sum(jnp.concatenate(rows, axis=0), axis=1, keepdims=True)
        codes[0:1, :] = jnp.sum(jnp.where(row == lane, each, 0), axis=0, keepdims=True)
        codes[1:8, :] = jnp.zeros((7, 128), jnp.int32)

    def find_tables():
        own = lax.broadcasted_iota(jnp.int32, (128, 128), 0).astype(F32) * inv_ref[...]
        trig[0], trig[1] = jnp.cos(own), jnp.sin(own)
        diagonal = lax.broadcasted_iota(jnp.int32, (64, 64), 0) == lax.broadcasted_iota(jnp.int32, (64, 64), 1)
        column = jnp.sum(jnp.where(diagonal, lens_ref[...], 0), axis=1, keepdims=True)
        start = column.astype(F32) * inv_ref[...]
        rtrig[0], rtrig[1] = jnp.cos(start), jnp.sin(start)

    local = [
        pltpu.make_async_copy(w_ref, w_slot(zh), lsem.at[0]),
        pltpu.make_async_copy(pages_ref.at[0], py.at[zh, x], lsem.at[1]),
        pltpu.make_async_copy(pages_ref.at[1], px.at[zh, y], lsem.at[2]),
        pltpu.make_async_copy(q_part(0), qy.at[y], lsem.at[3]),
        pltpu.make_async_copy(q_part(1), qx.at[x], lsem.at[4]),
    ]
    b = base[0]
    base[0] += 3
    r_across = remote(rows_ref, rows_all.at[tp], sems, b, across)
    r_partner = remote(rows_ref, rows_all.at[tp], sems, b + 1, partner)
    zp[0].start()
    zp[1].start()
    zw.start()
    r_partner.start()
    q_rings = [new(y, peer_y, q_part(0), lambda s: qy.at[s], 64),
               new(x, peer_x, q_part(1), lambda s: qx.at[s], 64)]
    p_own = [p_ring(0, 0), p_ring(0, 1)]
    w_own = w_ring(0)
    rings = [zw] + zp + q_rings + p_own + [w_own]
    for r in p_own + [w_own] + q_rings:
        r.start()
    for d in local:
        d.start()
    norm(rows_ref[...], tp)
    there = rows_all.at[2 * (1 - zl) + c]
    mine = rows_all.at[2 * zl + 1 - c]
    other = rows_all.at[2 * (1 - zl) + 1 - c]

    def step(ring):
        for r in (-1, 1):
            ring.arrived(r)
            ring.forward(r)

    late = []

    def begin(ring):
        ring.start()
        late.append(ring)
        return ring

    for r in p_own:
        step(r)
    p_near = []
    for r in (-1, 1):
        for h in (0, 1):
            zp[h].arrived(r)
            zp[h].forward(r)
            zp[h].rest(r)
            p_near.append(begin(p_ring(r, h)))
    step(w_own)
    for r in q_rings:
        step(r)
    for r in p_near:
        step(r)
    w_near = []
    for r in (-1, 1):
        zw.arrived(r)
        zw.forward(r)
        zw.rest(r)
        w_near.append(begin(w_ring(r)))
    r_across.start()
    remote(mine, mine, sems, b + 1, partner).wait_recv()
    norm(mine[...], 2 * zl + 1 - c)
    find_codes()
    find_tables()
    p_far = []
    for h in (0, 1):
        zp[h].far()
        p_far.append(begin(p_ring(2, h)))
    step(w_near[0])
    zw.far()
    w_far = begin(w_ring(2))
    step(w_near[1])
    for r in p_far:
        step(r)
    remote(there, there, sems, b, across).wait_recv()
    r_pass = remote(there, there, sems, b + 2, partner)
    r_pass.start()
    norm(there[...], 2 * (1 - zl) + c)
    step(w_far)
    remote(other, other, sems, b + 2, partner).wait_recv()
    norm(other[...], 2 * (1 - zl) + 1 - c)
    for ring in q_rings + p_own + [w_own] + late:
        ring.rest(-1)
        ring.rest(1)
        ring.far()
    for r in rings + late:
        r.drain()
    for d in (r_across, r_partner, r_pass):
        d.wait_send()
    for d in local:
        d.wait()
    assert base[0] <= NSEM, base[0]


NSEM = 112


def gather(rows, pages, q, w, gain, table, lens, inverse):
    s = jax.ShapeDtypeStruct
    vm = pl.BlockSpec(memory_space=pltpu.VMEM)
    return pl.pallas_call(
        gather_kernel,
        out_shape=(s((4, 32, 5120), BF), s((4, 4, 256, 128), BF), s((4, 4, 256, 128), BF),
                   s((4, 128, 640), BF), s((4, 128, 640), BF), s((2, 2, 4, 80, 1280), BF),
                   s((8, 128), jnp.int32), s((2, 128, 128), F32), s((2, 64, 128), F32)),
        in_specs=[vm] * 8,
        out_specs=[vm] + [pl.BlockSpec(memory_space=pl.ANY)] * 5 + [vm] * 3,
        scratch_shapes=[pltpu.VMEM((4, 32, 5120), BF), pltpu.SemaphoreType.DMA((2, NSEM)),
                        pltpu.SemaphoreType.DMA((5,))],
        compiler_params=pltpu.CompilerParams(collective_id=0, has_side_effects=True),
        name="gather",
    )(rows, pages, q, w, gain, table, lens, inverse)


NT = (((1,), (1,)), ((), ()))
TN = (((0,), (0,)), ((), ()))


def attend_kernel(codes, kvp_ref, bias_ref, qy_ref, qx_ref, py_ref, px_ref, trig_ref, rtrig_ref,
                  o_ref, st_ref, kv_ref, q_s, m_s, l_s, acc_s):
    y, zh, x, zl, c = coords()
    me = y * 16 + zh * 4 + x
    scale = LOG2E * 128 ** -0.5
    lane = lax.broadcasted_iota(jnp.int32, (1, 128), 1)
    sign = jnp.where(lane < 64, -1.0, 1.0).astype(F32)

    def trig(r):
        cl = rtrig_ref[0, pl.ds(r, 1), :]
        sl = rtrig_ref[1, pl.ds(r, 1), :]
        ct, st = trig_ref[0], trig_ref[1]
        return cl * ct - sl * st, (sl * ct + cl * st) * sign

    def rope(v, cs):
        return v * cs[0] + pltpu.roll(v, 64, 1) * cs[1]

    cs_own = trig(me)
    bias = bias_ref[...].astype(F32)
    for h in range(2):
        key = kvp_ref[0, :, h * 128:(h + 1) * 128] + bias[0:1, h * 128:(h + 1) * 128]
        kv_ref[:, h * 128:(h + 1) * 128] = rope(key, cs_own).astype(BF)
    kv_ref[:, 256:512] = (kvp_ref[1] + bias[1:2, :]).astype(BF)

    row = lax.broadcasted_iota(jnp.int32, (128, 640), 0)
    col = lax.broadcasted_iota(jnp.int32, (128, 640), 1)

    def update(key, value, keep):
        s = lax.dot_general(key, q_s[...], NT, preferred_element_type=F32) * scale
        s = jnp.where(keep, s, LOW)
        m_old = m_s[0:1, :]
        m_new = jnp.maximum(m_old, jnp.max(s, axis=0, keepdims=True))
        p = jnp.exp2(s - m_new)
        a = jnp.exp2(m_old - m_new)
        l_s[0:1, :] = l_s[0:1, :] * a + jnp.sum(p, axis=0, keepdims=True)
        m_s[0:1, :] = m_new
        acc_s[...] = acc_s[...] * a + lax.dot_general(value, p.astype(BF), TN, preferred_element_type=F32)

    for t in range(2):
        q_ref, p_ref = (qy_ref, py_ref) if t == 0 else (qx_ref, px_ref)
        mine = y if t == 0 else x

        def request_of(i, t=t):
            return i * 16 + zh * 4 + x if t == 0 else y * 16 + zh * 4 + i

        def page_of(s, t=t):
            return y * 16 + s if t == 0 else (s % 4) * 16 + (s // 4) * 4 + x

        def one(i, _, t=t, q_ref=q_ref, p_ref=p_ref, mine=mine, request_of=request_of, page_of=page_of):
            r = request_of(i)

            def count(s, n):
                code = codes[0, page_of(s)]
                return n + jnp.where((code // 256 == r) & (code % 256 > 0), 1, 0)

            pages = lax.fori_loop(0, 16, count, jnp.int32(0), unroll=True)
            active = (pages > 0) | (i == mine)
            m_s[...] = jnp.full_like(m_s, LOW)
            l_s[...] = jnp.zeros_like(l_s)

            @pl.when(active)
            def _():
                cs = trig(r)
                acc_s[...] = jnp.zeros_like(acc_s)
                for h in range(5):
                    v = q_ref[i, :, h * 128:(h + 1) * 128].astype(F32)
                    q_s[h * 128:(h + 1) * 128, :] = rope(v, cs).astype(BF)

                @pl.when(i == mine)
                def _():
                    update(kv_ref[:, t * 128:(t + 1) * 128], kv_ref[:, 256 + t * 128:384 + t * 128],
                           row <= col % 128)

                def visit(s, z):
                    code = codes[0, page_of(s)]
                    seen = code % 256

                    @pl.when((code // 256 == r) & (seen > 0))
                    def _():
                        update(p_ref[s, 0:128, :], p_ref[s, 128:256, :], row < seen)

                    return z

                lax.fori_loop(0, 16, visit, 0)
                o_ref[t, i] = (acc_s[...] / l_s[0:1, :]).astype(BF)

            @pl.when(jnp.logical_not(active))
            def _():
                o_ref[t, i] = jnp.zeros((128, 640), BF)

            st_ref[t, i, 0:1, :] = m_s[0:1, :]
            st_ref[t, i, 1:2, :] = l_s[0:1, :]
            return 0

        lax.fori_loop(0, 4, one, 0)


def attend(codes, kvp, bias, qy, qx, py, px, trig, rtrig):
    s = jax.ShapeDtypeStruct
    vm = pl.BlockSpec(memory_space=pltpu.VMEM)
    sm = pl.BlockSpec(memory_space=pltpu.SMEM)
    return pl.pallas_call(
        attend_kernel,
        out_shape=(s((2, 4, 128, 640), BF), s((2, 4, 8, 640), F32), s((128, 512), BF)),
        in_specs=[sm] + [vm] * 8,
        out_specs=[vm] * 3,
        scratch_shapes=[pltpu.VMEM((640, 128), BF), pltpu.VMEM((8, 640), F32), pltpu.VMEM((8, 640), F32),
                        pltpu.VMEM((128, 640), F32)],
        name="attend",
    )(codes, kvp, bias, qy, qx, py.reshape(16, 256, 128), px.reshape(16, 256, 128), trig, rtrig)


def project_kernel(o_ref, st_ref, w4_ref, out_ref, fin, wv, ro, rst, relay, att, ay, ax, part, rc, ps, ra, tot, sems, wsem):
    y, zh, x, zl, c = coords()
    partner = (y, zh, x, zl, 1 - c)
    across = (y, zh, x, 1 - zl, c)
    near = [shifted(a, b) for a in (0, 2) for b in (1, -1, 2)] + [partner, across]
    load = [pltpu.make_async_copy(w4_ref.at[t], wv.at[t], wsem.at[t]) for t in range(2)]
    for d in load:
        d.start()
    barrier = pltpu.get_barrier_semaphore()
    for d in near:
        pl.semaphore_signal(barrier, inc=1, device_id=d, device_id_type=MESH)
    pl.semaphore_wait(barrier, len(near))

    axes = (0, 2)
    mine = (y, x)
    sent = []
    base = [0]

    def send(src, dst, n, device):
        d = remote(src, dst, sems, n, device)
        d.start()
        sent.append(d)

    def got(dst, n):
        remote(dst, dst, sems, n, partner).wait_recv()

    def take(n):
        base[0] += n
        return base[0] - n

    slot = lambda t, r: lax.rem(mine[t] + r + 4, 4)
    d0 = [take(9), take(9)]
    for t in range(2):
        far = o_ref.at[t, slot(t, 2)]
        for h, by in ((0, 1), (1, -1)):
            send(far.at[pl.ds(h * 64, 64)], relay.at[t, h], d0[t] + h, shifted(axes[t], by))
    for t in range(2):
        for h, by in ((0, 1), (1, -1)):
            send(st_ref.at[t, slot(t, by)], rst.at[t, h], d0[t] + 2 + h, shifted(axes[t], by))
        send(st_ref.at[t, slot(t, 2)], rst.at[t, 2], d0[t] + 4, shifted(axes[t], 2))
        for h, by in ((0, 1), (1, -1)):
            send(o_ref.at[t, slot(t, by)], ro.at[t, h], d0[t] + 5 + h, shifted(axes[t], by))
    for t in range(2):
        for h, by in ((0, 1), (1, -1)):
            got(relay.at[t, h], d0[t] + h)
            send(relay.at[t, h], ro.at[t, 2, pl.ds(h * 64, 64)], d0[t] + 7 + h, shifted(axes[t], by))
    for t in range(2):
        for h in (0, 1):
            got(rst.at[t, h], d0[t] + 2 + h)
            got(ro.at[t, h], d0[t] + 5 + h)
            got(ro.at[t, 2, pl.ds(h * 64, 64)], d0[t] + 7 + h)
        got(rst.at[t, 2], d0[t] + 4)
    for t in range(2):
        own = slot(t, 0)
        ms = [st_ref[t, own, 0:1, :]] + [rst[t, i, 0:1, :] for i in range(3)]
        ls = [st_ref[t, own, 1:2, :]] + [rst[t, i, 1:2, :] for i in range(3)]
        top = jnp.maximum(jnp.maximum(ms[0], ms[1]), jnp.maximum(ms[2], ms[3]))
        es = [jnp.exp2(m - top) * l for m, l in zip(ms, ls)]
        inv = 1.0 / (es[0] + es[1] + es[2] + es[3])
        mixed = o_ref[t, own].astype(F32) * (es[0] * inv)
        for i in range(3):
            mixed = mixed + ro[t, i].astype(F32) * (es[i + 1] * inv)
        for h in range(5):
            att[:, (t * 5 + h) * 128:(t * 5 + h + 1) * 128] = mixed[:, h * 128:(h + 1) * 128].T.astype(BF)

    bufs = (ay, ax)
    rings = []
    for t in range(2):
        rings.append(Ring(mine[t], functools.partial(shifted, axes[t]), att, (lambda s, t=t: bufs[t].at[s]), 64,
                          sems, take(6)))
        rings[t].start()
    for d in load:
        d.wait()
    g1, g2, g3 = take(8), take(8), take(8)
    order = (0, -1, 1, 2)

    def multiply(k):
        for t in range(2):
            s = slot(t, order[k])
            a = att[...] if k == 0 else bufs[t][s]
            res = lax.dot_general(a, wv[t].reshape(640, 1280), NT, preferred_element_type=F32).astype(BF)
            for z in range(2):
                for cc in range(2):
                    n = 2 * z + cc
                    part[t, k, cc, z] = res[32 * n:32 * n + 32, :]
            send(part.at[t, k, 1 - c], rc.at[t, k], g1 + 2 * k + t, partner)

    def pair(k):
        for t in range(2):
            got(rc.at[t, k], g1 + 2 * k + t)
            v = part[t, k, c, 1 - zl].astype(F32) + rc[t, k, 1 - zl].astype(F32)
            ps[t, k] = v.astype(BF)
            send(ps.at[t, k], ra.at[t, k], g2 + 2 * k + t, across)

    def finish(k):
        for t in range(2):
            got(ra.at[t, k], g2 + 2 * k + t)
            v = part[t, k, c, zl].astype(F32) + rc[t, k, zl].astype(F32) + ra[t, k].astype(F32)
            if k == 0:
                fin[t, mine[t]] = v.astype(BF)
            else:
                tot[t, k] = v.astype(BF)
                send(tot.at[t, k], fin.at[t, mine[t]], g3 + 2 * k + t, shifted(axes[t], order[k]))

    multiply(0)
    for r in (-1, 1):
        for ring in rings:
            ring.arrived(r)
            ring.forward(r)
    pair(0)
    for ring in rings:
        ring.rest(-1)
    multiply(1)
    pair(1)
    for ring in rings:
        ring.rest(1)
    multiply(2)
    pair(2)
    finish(0)
    finish(1)
    for ring in rings:
        ring.far()
    multiply(3)
    finish(2)
    pair(3)
    finish(3)
    for t in range(2):
        for k in (1, 2, 3):
            got(fin.at[t, slot(t, -order[k])], g3 + 2 * k + t)
    for u in range(4):
        for g in range(2):
            pieces = [fin[0, u].astype(F32)[:, g * 320:g * 320 + 320]]
            for s in range(4):
                first = g * 320 + u * 80
                pieces.append(fin[1, s].astype(F32)[:, first:first + 80])
            cols = pl.ds(u * 1280 + g * 640, 640)
            out_ref[:, cols] = jnp.concatenate(pieces, axis=1).astype(BF)
    for d in sent:
        d.wait_send()
    for ring in rings:
        ring.drain()
    assert base[0] <= NSEM3, base[0]


NSEM3 = 56


def project(o, st, w4):
    s = jax.ShapeDtypeStruct
    vm = pl.BlockSpec(memory_space=pltpu.VMEM)
    return pl.pallas_call(
        project_kernel,
        out_shape=s((32, 5120), BF),
        in_specs=[vm, vm, pl.BlockSpec(memory_space=pl.ANY)],
        out_specs=vm,
        scratch_shapes=[
            pltpu.VMEM((2, 4, 32, 640), BF),
            pltpu.VMEM((2, 2, 4, 80, 1280), BF), pltpu.VMEM((2, 3, 128, 640), BF), pltpu.VMEM((2, 3, 8, 640), F32),
            pltpu.VMEM((2, 2, 64, 640), BF), pltpu.VMEM((128, 1280), BF), pltpu.VMEM((4, 128, 1280), BF),
            pltpu.VMEM((4, 128, 1280), BF), pltpu.VMEM((2, 4, 2, 2, 32, 640), BF), pltpu.VMEM((2, 4, 2, 32, 640), BF),
            pltpu.VMEM((2, 4, 32, 640), BF), pltpu.VMEM((2, 4, 32, 640), BF), pltpu.VMEM((2, 4, 32, 640), BF),
            pltpu.SemaphoreType.DMA((2, NSEM3)), pltpu.SemaphoreType.DMA((2,))],
        compiler_params=pltpu.CompilerParams(collective_id=1, has_side_effects=True),
        name="project",
    )(o, st, w4)


def local(hidden_in, norm_gain, kv_weight, kv_bias, queries, cache_pages, out_weight, cached_len, page_table):
    pages = cache_pages[0].transpose(2, 1, 0, 3).reshape(2, 256, 128)
    pair = lax.broadcasted_iota(jnp.int32, (1, 128), 1) % 64
    inverse = jnp.power(THETA, -pair.astype(F32) * 2.0 / 128)
    normed, py, px, qy, qx, w4, codes, trig, rtrig = gather(
        hidden_in, pages, queries, out_weight.T, norm_gain.reshape(40, 128),
        page_table.T, cached_len.reshape(1, 64), inverse)
    kvp = jnp.einsum("td,dsc->stc", normed.reshape(128, 5120), kv_weight, preferred_element_type=F32)
    o, st, kv = attend(codes, kvp, kv_bias, qy, qx, py, px, trig, rtrig)
    summed = project(o, st, w4)
    hidden_out = (hidden_in.astype(F32) + summed.astype(F32)).astype(BF)
    return hidden_out, kv.reshape(128, 2, 2, 128)


def solution(mesh):
    fine = Mesh(mesh.devices.reshape(4, 4, 4, 2, 2), ("y", "zh", "x", "zl", "c"))
    blk, tp = ("y", "zh", "x"), ("zl", "c")
    in_specs = (P(blk + tp, None), P(), P(None, None, tp), P(None, tp), P(blk, tp),
                P(blk, None, None, tp, None), P(tp, blk), P(), P())
    out_specs = (P(blk + tp, None), P(blk, None, tp, None))
    return jax.shard_map(local, mesh=fine, in_specs=in_specs, out_specs=out_specs, check_vma=False)
```

```python
import functools

import jax
import jax.numpy as jnp
from jax import lax
from jax.experimental import pallas as pl
from jax.experimental.pallas import tpu as pltpu
from jax.sharding import Mesh, PartitionSpec as P

EPS = 1e-06
THETA = 1000000.0
LOW = -1e30
LOG2E = 1.4426950408889634
MESH = pl.DeviceIdType.MESH
HBM = pl.ANY
BF = jnp.bfloat16
F32 = jnp.float32


def coords():
    return tuple(lax.axis_index(a) for a in ("y", "zh", "x", "zl", "c"))


def shifted(axis, by):
    me = list(coords())
    me[axis] = lax.rem(me[axis] + by + 4, 4)
    return tuple(me)


def remote(src, dst, sems, n, device):
    return pltpu.make_async_remote_copy(
        src_ref=src, dst_ref=dst, send_sem=sems.at[0, n], recv_sem=sems.at[1, n],
        device_id=device, device_id_type=MESH)


class Ring:
    def __init__(self, me, peer, own, at, half, sems, base):
        self.me, self.peer, self.own, self.at, self.half = me, peer, own, at, half
        self.sems, self.base = sems, base
        self.sent = []

    def slot(self, r):
        return lax.rem(self.me + r + 4, 4)

    def part(self, s, h):
        return self.at(s).at[pl.ds(h * self.half, self.half)]

    def start(self):
        for second in (0, 1):
            for n, by in ((0, 1), (1, -1)):
                h = n ^ second
                src = self.own.at[pl.ds(h * self.half, self.half)]
                d = remote(src, self.part(self.me, h), self.sems, self.base + 4 * second + n, self.peer(by))
                d.start()
                self.sent.append(d)

    def landed(self, r, second):
        n = 0 if r == -1 else 1
        s = self.part(self.slot(r), n ^ second)
        remote(s, s, self.sems, self.base + 4 * second + n, self.peer(1)).wait_recv()

    def arrived(self, r):
        self.landed(r, 0)

    def rest(self, r):
        self.landed(r, 1)

    def forward(self, r):
        h = 0 if r == -1 else 1
        s = self.part(self.slot(r), h)
        d = remote(s, s, self.sems, self.base + 2 + h, self.peer(-r))
        d.start()
        self.sent.append(d)

    def far(self):
        for h in (0, 1):
            s = self.part(self.slot(2), h)
            remote(s, s, self.sems, self.base + 2 + h, self.peer(1)).wait_recv()

    def drain(self):
        for d in self.sent:
            d.wait_send()


def gather_kernel(rows_ref, pages_ref, q_ref, w_ref, gain_ref, table_ref, lens_ref, inv_ref, normed, py, px, qy, qx, w4,
                  codes, trig, rtrig, rows_all, sems, lsem):
    y, zh, x, zl, c = coords()
    partner = (y, zh, x, zl, 1 - c)
    across = (y, zh, x, 1 - zl, c)
    barrier = pltpu.get_barrier_semaphore()
    near = [shifted(a, b) for a in (0, 1, 2) for b in (1, -1)] + [partner, across]
    for d in near:
        pl.semaphore_signal(barrier, inc=1, device_id=d, device_id_type=MESH)
    pl.semaphore_wait(barrier, len(near))

    tp = 2 * zl + c
    base = [0]

    def new(me, peer, own, at, half, count=6):
        r = Ring(me, peer, own, at, half, sems, base[0])
        base[0] += count
        return r

    peer_z = lambda by: shifted(1, by)
    peer_y = lambda by: shifted(0, by)
    peer_x = lambda by: shifted(2, by)

    def w_slot(i):
        t = lax.rem(i, 2)
        return w4.at[t, i // 2, x * (1 - t) + y * t]

    def w_ring(r):
        i = lax.rem(zh + r + 4, 4)
        t = lax.rem(i, 2)
        def peer(by):
            return (lax.rem(y + t * by + 4, 4), zh, lax.rem(x + (1 - t) * by + 4, 4), zl, c)
        own = w_ref if r == 0 else w_slot(i)
        return new(x * (1 - t) + y * t, peer, own, lambda s: w4.at[t, i // 2, s], 40)

    def p_ring(r, head):
        i = lax.rem(zh + r + 4, 4)
        buf = px if head else py
        me = y if head else x
        own = pages_ref.at[head] if r == 0 else buf.at[i, me]
        return new(me, peer_y if head else peer_x, own, lambda s: buf.at[i, s], 128)

    zw = new(zh, peer_z, w_ref, w_slot, 40)
    zp = [new(zh, peer_z, pages_ref.at[h], (lambda i: px.at[i, y]) if h else (lambda i: py.at[i, x]), 128)
          for h in (0, 1)]
    def q_part(t):
        return q_ref.at[:, pl.ds(t * 640, 640)]

    def norm(block, slot):
        v = block.astype(F32)
        inverse_rms = lax.rsqrt(jnp.mean(v * v, axis=-1, keepdims=True) + EPS)
        v = v * inverse_rms
        for k in range(40):
            cols = pl.ds(k * 128, 128)
            normed[slot, :, cols] = (v[:, k * 128:k * 128 + 128] * gain_ref[k:k + 1, :].astype(F32)).astype(BF)

    def find_codes():
        table = table_ref[...]
        r = lax.broadcasted_iota(jnp.int32, (32, 64), 1)
        j = lax.broadcasted_iota(jnp.int32, (32, 64), 0)
        seen = jnp.clip(lens_ref[...] - j * 128, 0, 128)
        value = jnp.where(seen > 0, r * 256 + seen, 0)
        row = lax.broadcasted_iota(jnp.int32, (64, 128), 0)
        lane = lax.broadcasted_iota(jnp.int32, (64, 128), 1)
        rows = [jnp.sum(jnp.where(table == p, value, 0), axis=0, keepdims=True) for p in range(64)]
        each = jnp.sum(jnp.concatenate(rows, axis=0), axis=1, keepdims=True)
        codes[0:1, :] = jnp.sum(jnp.where(row == lane, each, 0), axis=0, keepdims=True)
        codes[1:8, :] = jnp.zeros((7, 128), jnp.int32)

    def find_tables():
        own = lax.broadcasted_iota(jnp.int32, (128, 128), 0).astype(F32) * inv_ref[...]
        trig[0], trig[1] = jnp.cos(own), jnp.sin(own)
        diagonal = lax.broadcasted_iota(jnp.int32, (64, 64), 0) == lax.broadcasted_iota(jnp.int32, (64, 64), 1)
        column = jnp.sum(jnp.where(diagonal, lens_ref[...], 0), axis=1, keepdims=True)
        start = column.astype(F32) * inv_ref[...]
        rtrig[0], rtrig[1] = jnp.cos(start), jnp.sin(start)

    local = [
        pltpu.make_async_copy(w_ref, w_slot(zh), lsem.at[0]),
        pltpu.make_async_copy(pages_ref.at[0], py.at[zh, x], lsem.at[1]),
        pltpu.make_async_copy(pages_ref.at[1], px.at[zh, y], lsem.at[2]),
        pltpu.make_async_copy(q_part(0), qy.at[y], lsem.at[3]),
        pltpu.make_async_copy(q_part(1), qx.at[x], lsem.at[4]),
    ]
    b = base[0]
    base[0] += 3
    r_across = remote(rows_ref, rows_all.at[tp], sems, b, across)
    r_partner = remote(rows_ref, rows_all.at[tp], sems, b + 1, partner)
    zp[0].start()
    zp[1].start()
    zw.start()
    r_partner.start()
    q_rings = [new(y, peer_y, q_part(0), lambda s: qy.at[s], 64),
               new(x, peer_x, q_part(1), lambda s: qx.at[s], 64)]
    p_own = [p_ring(0, 0), p_ring(0, 1)]
    w_own = w_ring(0)
    rings = [zw] + zp + q_rings + p_own + [w_own]
    for r in p_own + [w_own] + q_rings:
        r.start()
    for d in local:
        d.start()
    norm(rows_ref[...], tp)
    there = rows_all.at[2 * (1 - zl) + c]
    mine = rows_all.at[2 * zl + 1 - c]
    other = rows_all.at[2 * (1 - zl) + 1 - c]

    def step(ring):
        for r in (-1, 1):
            ring.arrived(r)
            ring.forward(r)

    late = []

    def begin(ring):
        ring.start()
        late.append(ring)
        return ring

    for r in p_own:
        step(r)
    p_near = []
    for r in (-1, 1):
        for h in (0, 1):
            zp[h].arrived(r)
            zp[h].forward(r)
            zp[h].rest(r)
            p_near.append(begin(p_ring(r, h)))
    step(w_own)
    for r in q_rings:
        step(r)
    for r in p_near:
        step(r)
    w_near = []
    for r in (-1, 1):
        zw.arrived(r)
        zw.forward(r)
        zw.rest(r)
        w_near.append(begin(w_ring(r)))
    r_across.start()
    remote(mine, mine, sems, b + 1, partner).wait_recv()
    norm(mine[...], 2 * zl + 1 - c)
    find_codes()
    find_tables()
    p_far = []
    for h in (0, 1):
        zp[h].far()
        p_far.append(begin(p_ring(2, h)))
    step(w_near[0])
    zw.far()
    w_far = begin(w_ring(2))
    step(w_near[1])
    for r in p_far:
        step(r)
    remote(there, there, sems, b, across).wait_recv()
    r_pass = remote(there, there, sems, b + 2, partner)
    r_pass.start()
    norm(there[...], 2 * (1 - zl) + c)
    step(w_far)
    remote(other, other, sems, b + 2, partner).wait_recv()
    norm(other[...], 2 * (1 - zl) + 1 - c)
    for ring in q_rings + p_own + [w_own] + late:
        ring.rest(-1)
        ring.rest(1)
        ring.far()
    for r in rings + late:
        r.drain()
    for d in (r_across, r_partner, r_pass):
        d.wait_send()
    for d in local:
        d.wait()
    assert base[0] <= NSEM, base[0]


NSEM = 112


def gather(rows, pages, q, w, gain, table, lens, inverse):
    s = jax.ShapeDtypeStruct
    vm = pl.BlockSpec(memory_space=pltpu.VMEM)
    return pl.pallas_call(
        gather_kernel,
        out_shape=(s((4, 32, 5120), BF), s((4, 4, 256, 128), BF), s((4, 4, 256, 128), BF),
                   s((4, 128, 640), BF), s((4, 128, 640), BF), s((2, 2, 4, 80, 1280), BF),
                   s((8, 128), jnp.int32), s((2, 128, 128), F32), s((2, 64, 128), F32)),
        in_specs=[vm] * 8,
        out_specs=[vm] + [pl.BlockSpec(memory_space=pl.ANY)] * 5 + [vm] * 3,
        scratch_shapes=[pltpu.VMEM((4, 32, 5120), BF), pltpu.SemaphoreType.DMA((2, NSEM)),
                        pltpu.SemaphoreType.DMA((5,))],
        compiler_params=pltpu.CompilerParams(collective_id=0, has_side_effects=True, vmem_limit_bytes=12 * 2**20),
        name="gather",
    )(rows, pages, q, w, gain, table, lens, inverse)


NT = (((1,), (1,)), ((), ()))
TN = (((0,), (0,)), ((), ()))


def attend_kernel(codes, kvp_ref, bias_ref, qy_ref, qx_ref, py_ref, px_ref, trig_ref, rtrig_ref,
                  o_ref, st_ref, kv_ref, q_s, m_s, l_s, acc_s):
    y, zh, x, zl, c = coords()
    me = y * 16 + zh * 4 + x
    scale = LOG2E * 128 ** -0.5
    lane = lax.broadcasted_iota(jnp.int32, (1, 128), 1)
    sign = jnp.where(lane < 64, -1.0, 1.0).astype(F32)

    def trig(r):
        cl = rtrig_ref[0, pl.ds(r, 1), :]
        sl = rtrig_ref[1, pl.ds(r, 1), :]
        ct, st = trig_ref[0], trig_ref[1]
        return cl * ct - sl * st, (sl * ct + cl * st) * sign

    def rope(v, cs):
        return v * cs[0] + pltpu.roll(v, 64, 1) * cs[1]

    cs_own = trig(me)
    bias = bias_ref[...].astype(F32)
    for h in range(2):
        key = kvp_ref[0, :, h * 128:(h + 1) * 128] + bias[0:1, h * 128:(h + 1) * 128]
        kv_ref[:, h * 128:(h + 1) * 128] = rope(key, cs_own).astype(BF)
    kv_ref[:, 256:512] = (kvp_ref[1] + bias[1:2, :]).astype(BF)

    row = lax.broadcasted_iota(jnp.int32, (128, 640), 0)
    col = lax.broadcasted_iota(jnp.int32, (128, 640), 1)

    def update(key, value, keep):
        s = lax.dot_general(key, q_s[...], NT, preferred_element_type=F32) * scale
        s = jnp.where(keep, s, LOW)
        m_old = m_s[0:1, :]
        m_new = jnp.maximum(m_old, jnp.max(s, axis=0, keepdims=True))
        p = jnp.exp2(s - m_new)
        a = jnp.exp2(m_old - m_new)
        l_s[0:1, :] = l_s[0:1, :] * a + jnp.sum(p, axis=0, keepdims=True)
        m_s[0:1, :] = m_new
        acc_s[...] = acc_s[...] * a + lax.dot_general(value, p.astype(BF), TN, preferred_element_type=F32)

    for t in range(2):
        q_ref, p_ref = (qy_ref, py_ref) if t == 0 else (qx_ref, px_ref)
        mine = y if t == 0 else x

        def request_of(i, t=t):
            return i * 16 + zh * 4 + x if t == 0 else y * 16 + zh * 4 + i

        def page_of(s, t=t):
            return y * 16 + s if t == 0 else (s % 4) * 16 + (s // 4) * 4 + x

        def one(i, _, t=t, q_ref=q_ref, p_ref=p_ref, mine=mine, request_of=request_of, page_of=page_of):
            r = request_of(i)

            def count(s, n):
                code = codes[0, page_of(s)]
                return n + jnp.where((code // 256 == r) & (code % 256 > 0), 1, 0)

            pages = lax.fori_loop(0, 16, count, jnp.int32(0), unroll=True)
            active = (pages > 0) | (i == mine)
            m_s[...] = jnp.full_like(m_s, LOW)
            l_s[...] = jnp.zeros_like(l_s)

            @pl.when(active)
            def _():
                cs = trig(r)
                acc_s[...] = jnp.zeros_like(acc_s)
                for h in range(5):
                    v = q_ref[i, :, h * 128:(h + 1) * 128].astype(F32)
                    q_s[h * 128:(h + 1) * 128, :] = rope(v, cs).astype(BF)

                @pl.when(i == mine)
                def _():
                    update(kv_ref[:, t * 128:(t + 1) * 128], kv_ref[:, 256 + t * 128:384 + t * 128],
                           row <= col % 128)

                def visit(s, z):
                    code = codes[0, page_of(s)]
                    seen = code % 256

                    @pl.when((code // 256 == r) & (seen > 0))
                    def _():
                        update(p_ref[s, 0:128, :], p_ref[s, 128:256, :], row < seen)

                    return z

                lax.fori_loop(0, 16, visit, 0)
                o_ref[t, i] = (acc_s[...] / l_s[0:1, :]).astype(BF)

            @pl.when(jnp.logical_not(active))
            def _():
                o_ref[t, i] = jnp.zeros((128, 640), BF)

            st_ref[t, i, 0:1, :] = m_s[0:1, :]
            st_ref[t, i, 1:2, :] = l_s[0:1, :]
            return 0

        lax.fori_loop(0, 4, one, 0)


def attend(codes, kvp, bias, qy, qx, py, px, trig, rtrig):
    s = jax.ShapeDtypeStruct
    vm = pl.BlockSpec(memory_space=pltpu.VMEM)
    sm = pl.BlockSpec(memory_space=pltpu.SMEM)
    return pl.pallas_call(
        attend_kernel,
        out_shape=(s((2, 4, 128, 640), BF), s((2, 4, 8, 640), F32), s((128, 512), BF)),
        in_specs=[sm] + [vm] * 8,
        out_specs=[vm] * 3,
        scratch_shapes=[pltpu.VMEM((640, 128), BF), pltpu.VMEM((8, 640), F32), pltpu.VMEM((8, 640), F32),
                        pltpu.VMEM((128, 640), F32)],
        compiler_params=pltpu.CompilerParams(vmem_limit_bytes=16 * 2**20),
        name="attend",
    )(codes, kvp, bias, qy, qx, py.reshape(16, 256, 128), px.reshape(16, 256, 128), trig, rtrig)


def project_kernel(o_ref, st_ref, w4_ref, out_ref, fin, wv, ro, rst, relay, att, ay, ax, part, rc, ps, ra, tot, sems, wsem):
    y, zh, x, zl, c = coords()
    partner = (y, zh, x, zl, 1 - c)
    across = (y, zh, x, 1 - zl, c)
    near = [shifted(a, b) for a in (0, 2) for b in (1, -1, 2)] + [partner, across]
    load = [pltpu.make_async_copy(w4_ref.at[t], wv.at[t], wsem.at[t]) for t in range(2)]
    for d in load:
        d.start()
    barrier = pltpu.get_barrier_semaphore()
    for d in near:
        pl.semaphore_signal(barrier, inc=1, device_id=d, device_id_type=MESH)
    pl.semaphore_wait(barrier, len(near))

    axes = (0, 2)
    mine = (y, x)
    sent = []
    base = [0]

    def send(src, dst, n, device):
        d = remote(src, dst, sems, n, device)
        d.start()
        sent.append(d)

    def got(dst, n):
        remote(dst, dst, sems, n, partner).wait_recv()

    def take(n):
        base[0] += n
        return base[0] - n

    slot = lambda t, r: lax.rem(mine[t] + r + 4, 4)
    d0 = [take(9), take(9)]
    for t in range(2):
        far = o_ref.at[t, slot(t, 2)]
        for h, by in ((0, 1), (1, -1)):
            send(far.at[pl.ds(h * 64, 64)], relay.at[t, h], d0[t] + h, shifted(axes[t], by))
    for t in range(2):
        for h, by in ((0, 1), (1, -1)):
            send(st_ref.at[t, slot(t, by)], rst.at[t, h], d0[t] + 2 + h, shifted(axes[t], by))
        send(st_ref.at[t, slot(t, 2)], rst.at[t, 2], d0[t] + 4, shifted(axes[t], 2))
        for h, by in ((0, 1), (1, -1)):
            send(o_ref.at[t, slot(t, by)], ro.at[t, h], d0[t] + 5 + h, shifted(axes[t], by))
    for t in range(2):
        for h, by in ((0, 1), (1, -1)):
            got(relay.at[t, h], d0[t] + h)
            send(relay.at[t, h], ro.at[t, 2, pl.ds(h * 64, 64)], d0[t] + 7 + h, shifted(axes[t], by))
    for t in range(2):
        for h in (0, 1):
            got(rst.at[t, h], d0[t] + 2 + h)
            got(ro.at[t, h], d0[t] + 5 + h)
            got(ro.at[t, 2, pl.ds(h * 64, 64)], d0[t] + 7 + h)
        got(rst.at[t, 2], d0[t] + 4)
    for t in range(2):
        own = slot(t, 0)
        ms = [st_ref[t, own, 0:1, :]] + [rst[t, i, 0:1, :] for i in range(3)]
        ls = [st_ref[t, own, 1:2, :]] + [rst[t, i, 1:2, :] for i in range(3)]
        top = jnp.maximum(jnp.maximum(ms[0], ms[1]), jnp.maximum(ms[2], ms[3]))
        es = [jnp.exp2(m - top) * l for m, l in zip(ms, ls)]
        inv = 1.0 / (es[0] + es[1] + es[2] + es[3])
        mixed = o_ref[t, own].astype(F32) * (es[0] * inv)
        for i in range(3):
            mixed = mixed + ro[t, i].astype(F32) * (es[i + 1] * inv)
        for h in range(5):
            att[:, (t * 5 + h) * 128:(t * 5 + h + 1) * 128] = mixed[:, h * 128:(h + 1) * 128].T.astype(BF)

    bufs = (ay, ax)
    rings = []
    for t in range(2):
        rings.append(Ring(mine[t], functools.partial(shifted, axes[t]), att, (lambda s, t=t: bufs[t].at[s]), 64,
                          sems, take(6)))
        rings[t].start()
    for d in load:
        d.wait()
    g1, g2, g3 = take(8), take(8), take(8)
    order = (0, -1, 1, 2)

    def multiply(k):
        for t in range(2):
            s = slot(t, order[k])
            a = att[...] if k == 0 else bufs[t][s]
            res = lax.dot_general(a, wv[t].reshape(640, 1280), NT, preferred_element_type=F32).astype(BF)
            for z in range(2):
                for cc in range(2):
                    n = 2 * z + cc
                    part[t, k, cc, z] = res[32 * n:32 * n + 32, :]
            send(part.at[t, k, 1 - c], rc.at[t, k], g1 + 2 * k + t, partner)

    def pair(k):
        for t in range(2):
            got(rc.at[t, k], g1 + 2 * k + t)
            v = part[t, k, c, 1 - zl].astype(F32) + rc[t, k, 1 - zl].astype(F32)
            ps[t, k] = v.astype(BF)
            send(ps.at[t, k], ra.at[t, k], g2 + 2 * k + t, across)

    def finish(k):
        for t in range(2):
            got(ra.at[t, k], g2 + 2 * k + t)
            v = part[t, k, c, zl].astype(F32) + rc[t, k, zl].astype(F32) + ra[t, k].astype(F32)
            if k == 0:
                fin[t, mine[t]] = v.astype(BF)
            else:
                tot[t, k] = v.astype(BF)
                send(tot.at[t, k], fin.at[t, mine[t]], g3 + 2 * k + t, shifted(axes[t], order[k]))

    multiply(0)
    for r in (-1, 1):
        for ring in rings:
            ring.arrived(r)
            ring.forward(r)
    pair(0)
    for ring in rings:
        ring.rest(-1)
    multiply(1)
    pair(1)
    for ring in rings:
        ring.rest(1)
    multiply(2)
    pair(2)
    finish(0)
    finish(1)
    for ring in rings:
        ring.far()
    multiply(3)
    finish(2)
    pair(3)
    finish(3)
    for t in range(2):
        for k in (1, 2, 3):
            got(fin.at[t, slot(t, -order[k])], g3 + 2 * k + t)
    for u in range(4):
        for g in range(2):
            pieces = [fin[0, u].astype(F32)[:, g * 320:g * 320 + 320]]
            for s in range(4):
                first = g * 320 + u * 80
                pieces.append(fin[1, s].astype(F32)[:, first:first + 80])
            cols = pl.ds(u * 1280 + g * 640, 640)
            out_ref[:, cols] = jnp.concatenate(pieces, axis=1).astype(BF)
    for d in sent:
        d.wait_send()
    for ring in rings:
        ring.drain()
    assert base[0] <= NSEM3, base[0]


NSEM3 = 56


def project(o, st, w4):
    s = jax.ShapeDtypeStruct
    vm = pl.BlockSpec(memory_space=pltpu.VMEM)
    return pl.pallas_call(
        project_kernel,
        out_shape=s((32, 5120), BF),
        in_specs=[vm, vm, pl.BlockSpec(memory_space=pl.ANY)],
        out_specs=vm,
        scratch_shapes=[
            pltpu.VMEM((2, 4, 32, 640), BF),
            pltpu.VMEM((2, 2, 4, 80, 1280), BF), pltpu.VMEM((2, 3, 128, 640), BF), pltpu.VMEM((2, 3, 8, 640), F32),
            pltpu.VMEM((2, 2, 64, 640), BF), pltpu.VMEM((128, 1280), BF), pltpu.VMEM((4, 128, 1280), BF),
            pltpu.VMEM((4, 128, 1280), BF), pltpu.VMEM((2, 4, 2, 2, 32, 640), BF), pltpu.VMEM((2, 4, 2, 32, 640), BF),
            pltpu.VMEM((2, 4, 32, 640), BF), pltpu.VMEM((2, 4, 32, 640), BF), pltpu.VMEM((2, 4, 32, 640), BF),
            pltpu.SemaphoreType.DMA((2, NSEM3)), pltpu.SemaphoreType.DMA((2,))],
        compiler_params=pltpu.CompilerParams(collective_id=1, has_side_effects=True, vmem_limit_bytes=24 * 2**20),
        name="project",
    )(o, st, w4)


def local(hidden_in, norm_gain, kv_weight, kv_bias, queries, cache_pages, out_weight, cached_len, page_table):
    pages = cache_pages[0].transpose(2, 1, 0, 3).reshape(2, 256, 128)
    pair = lax.broadcasted_iota(jnp.int32, (1, 128), 1) % 64
    inverse = jnp.power(THETA, -pair.astype(F32) * 2.0 / 128)
    normed, py, px, qy, qx, w4, codes, trig, rtrig = gather(
        hidden_in, pages, queries, out_weight.T, norm_gain.reshape(40, 128),
        page_table.T, cached_len.reshape(1, 64), inverse)
    kvp = jnp.einsum("td,dsc->stc", normed.reshape(128, 5120), kv_weight, preferred_element_type=F32)
    o, st, kv = attend(codes, kvp, kv_bias, qy, qx, py, px, trig, rtrig)
    summed = project(o, st, w4)
    hidden_out = (hidden_in.astype(F32) + summed.astype(F32)).astype(BF)
    return hidden_out, kv.reshape(128, 2, 2, 128)


def solution(mesh):
    fine = Mesh(mesh.devices.reshape(4, 4, 4, 2, 2), ("y", "zh", "x", "zl", "c"))
    blk, tp = ("y", "zh", "x"), ("zl", "c")
    in_specs = (P(blk + tp, None), P(), P(None, None, tp), P(None, tp), P(blk, tp),
                P(blk, None, None, tp, None), P(tp, blk), P(), P())
    out_specs = (P(blk + tp, None), P(blk, None, tp, None))
    return jax.shard_map(local, mesh=fine, in_specs=in_specs, out_specs=out_specs, check_vma=False)
```
